32 devices in a mesh: tm: 4 (over y, x), space: 8 (over z, core).
Axes of the slice: x: 2, y: 2, z: 4, core: 2. Of those that a mesh axis runs over, the one named last changes fastest.
Arguments:
- queries: bfloat16 [4, 768, 3072], P('tm', 'space'), may hold values from -8 to 8
- key_rows: bfloat16 [4, 768, 3072], P('tm', 'space'), may hold values from -8 to 8
- value_rows: bfloat16 [4, 768, 3072], P('tm', 'space'), may hold values from -6 to 6
- noise_level: int32 [4], P('tm'), may hold values from 0 to 999
- decay_power: int32 [24], replicated, may hold values from 0 to 7
- head_gain: float32 [24, 128], replicated, may hold values from 0.1 to 1.9
Outputs:
- attended: bfloat16 [4, 768, 3072], P('tm', 'space')
The draws below stay inside these ranges and needn't reach their ends.
All inputs are finite; a program needn't handle non-finite values.
Results may differ from the reference program's by a relative error of at most 0.0049.
Values may be sent and summed in bfloat16 or wider, within the bound.
A program may use at most 64 MiB of HBM per device.

```python
import jax
import jax.numpy as jnp
from jax import lax

HEADS = 24
HD = 128
LEVELS = 1000
BLOCKS = 4
TOK_BLK = 768


def draw_entries(key):
    extent = (BLOCKS, TOK_BLK, HEADS * HD)
    query_key = jax.random.fold_in(key, 11)
    keys_key = jax.random.fold_in(key, 12)
    queries = jax.random.truncated_normal(query_key, -8.0, 8.0, extent, jnp.float32)
    keys_all = jax.random.truncated_normal(keys_key, -8.0, 8.0, extent, jnp.float32)
    return (queries, keys_all)


def draw_queries(key, part):
    return draw_entries(key)[0].astype(jnp.bfloat16)


def draw_key_rows(key, part):
    return draw_entries(key)[1].astype(jnp.bfloat16)


def touch_ends(array, stream_key, smallest, high):
    longest = array.shape.index(max(array.shape))
    spots = []
    for shift in (0, 1):
        where = [jax.random.randint(jax.random.fold_in(stream_key, axis), (), 0, length) for axis, length in enumerate(array.shape)]
        where[longest] = (where[longest] + shift) % array.shape[longest]
        spots.append(tuple(where))
    return array.at[spots[0]].set(smallest).at[spots[1]].set(high)


def block_scale(key, shape, pieces, least, high):
    def one(position, shards_of):
        heights = jax.random.uniform(jax.random.fold_in(jax.random.fold_in(key, 6), position), (shards_of,), jnp.float32, least / len(pieces), high / len(pieces))
        return jnp.repeat(jnp.exp(heights), shape[position] // shards_of).reshape((-1,) + (1,) * (len(shape) - position - 1))

    loudness = one(*pieces[0])
    for cut in pieces[1:]:
        loudness = loudness * one(*cut)
    return loudness


def gaussian(key, shape, scale, reach, shards=(), held_as=jnp.bfloat16):
    level = block_scale(key, shape, shards, -0.22, 0.18) if shards else 1.0
    entries = jax.random.normal(key, shape, jnp.float32) * scale * level
    return jnp.minimum(jnp.maximum(entries, -reach), reach).astype(held_as)


def setup_inputs(seed: int = 0) -> dict:
    key_list = jax.random.split(jax.random.key(seed), 7)
    return {
        "queries": draw_queries(jax.random.fold_in(key_list[6], 71), 0),
        "key_rows": draw_key_rows(jax.random.fold_in(key_list[6], 71), 0),
        "value_rows": gaussian(key_list[2], (BLOCKS, TOK_BLK, HEADS * HD), 1.0, 6.0, ((0, 4), (1, 8))),
        "noise_level": touch_ends(jax.random.randint(key_list[3], (BLOCKS,), 0, LEVELS), jax.random.fold_in(key_list[3], 1), 0, LEVELS - 1).astype(jnp.int32),
        "decay_power": touch_ends(jax.random.randint(key_list[4], (HEADS,), 0, 8), jax.random.fold_in(key_list[4], 1), 0, 7).astype(jnp.int32),
        "head_gain": jnp.clip(1.0 + 0.18 * jax.random.normal(key_list[5], (HEADS, HD), jnp.float32), 0.1, 1.9),
    }


epsilon = 1e-06

def attend_head(bundle):
    query, key_item, value_item, state, gain_row = bundle
    factor = query.shape[1] ** (-0.5)
    scores = jnp.dot(query, key_item.T, preferred_element_type=jnp.float32) * factor
    row_top = lax.optimization_barrier(jnp.max(scores, axis=1, keepdims=True))
    weights = jnp.exp(scores - row_top)
    row_total = lax.optimization_barrier(jnp.sum(weights, axis=1, keepdims=True))
    numerator = jnp.dot(weights.astype(jnp.bfloat16), value_item, preferred_element_type=jnp.float32)
    carried = jnp.dot(query, state, preferred_element_type=jnp.float32) * factor
    mixed = numerator / row_total + carried
    normed = mixed * lax.rsqrt(lax.optimization_barrier(jnp.mean(mixed * mixed, axis=1, keepdims=True)) + epsilon) * gain_row
    return normed.astype(jnp.bfloat16)

def outer_sum(bundle):
    key_head, value_head = bundle
    return jnp.dot(key_head.T, value_head, preferred_element_type=jnp.float32)

def by_heads(block):
    return block.reshape(TOK_BLK, HEADS, HD).transpose(1, 0, 2)

def reference(queries, key_rows, value_rows, noise_level, decay_power, head_gain):
    powers = decay_power.astype(jnp.float32)
    levels = noise_level.astype(jnp.float32)
    rates = jnp.exp2(-(powers[None, :] * (0.25 + 1.75 * levels[:, None] / LEVELS)) / BLOCKS)

    def one_block(carried_state, inputs):
        query_block, key_block, value_block, rate_now = inputs
        query_heads = by_heads(query_block)
        key_heads = by_heads(key_block)
        value_heads = by_heads(value_block)
        fresh = lax.map(outer_sum, (key_heads, value_heads)) / TOK_BLK
        state = (rate_now[:, None, None] * carried_state).astype(jnp.bfloat16)
        outcome = lax.map(attend_head, (query_heads, key_heads, value_heads, state, head_gain))
        advanced = rate_now[:, None, None] * carried_state + fresh
        return (advanced, outcome.transpose(1, 0, 2).reshape(TOK_BLK, HEADS * HD))
    start = jnp.zeros((HEADS, HD, HD), jnp.float32)
    unused_state, attended = lax.scan(one_block, start, (queries, key_rows, value_rows, rates))
    return attended
```

```python
import functools

import jax
import jax.numpy as jnp
from jax import lax
from jax.experimental import pallas as pl
from jax.experimental.pallas import tpu as pltpu
from jax.sharding import PartitionSpec as P

LEVELS = 1000
HGROUPS = 8
VMEM_GRANT = 32 * 2**20


epsilon = 1e-06


def carried_in(value, axis, join, neutral):
    count, mine = (lax.axis_size(axis), lax.axis_index(axis))
    pieces = jax.tree.map(lambda part: lax.all_gather(part, axis), value)
    so_far = jax.tree.map(
        lambda part, zero: jnp.full_like(part, 0) + jnp.asarray(zero, part.dtype), value, neutral
    )

    def lap(position, so_far):
        longer = join(so_far, jax.tree.map(lambda part: part[position], pieces))
        return jax.tree.map(lambda new, old: jnp.where(position < mine, new, old), longer, so_far)

    return lax.fori_loop(0, count - 1, lap, so_far)


def spread_items(block, quarters, heads_total, depth):
    part_rows = block.shape[0] // quarters
    shaped = block.reshape(quarters, part_rows, heads_total, depth).transpose(0, 2, 1, 3)
    return shaped.reshape(quarters * heads_total, part_rows, depth)


def copied_items(block, quarters, heads_total, depth):
    every = block.reshape(block.shape[0], heads_total, depth).transpose(1, 0, 2)
    copied = jnp.broadcast_to(every[None], (quarters,) + every.shape)
    return copied.reshape(quarters * heads_total, block.shape[0], depth)


def attend_head(bundle):
    query, key_item, value_item, state, gain_row = bundle
    factor = query.shape[1] ** (-0.5)
    scores = jnp.dot(query, key_item.T, preferred_element_type=jnp.float32) * factor
    row_top = jnp.max(scores, axis=1, keepdims=True)
    weights = jnp.exp(scores - row_top)
    row_total = jnp.sum(weights, axis=1, keepdims=True)
    numerator = jnp.dot(
        weights.astype(jnp.bfloat16), value_item, preferred_element_type=jnp.float32
    )
    carried = jnp.dot(query, state, preferred_element_type=jnp.float32) * factor
    mixed = numerator / row_total + carried
    normed = mixed * lax.rsqrt(jnp.mean(mixed * mixed, axis=1, keepdims=True) + epsilon) * gain_row
    return normed.astype(jnp.bfloat16)


def compose(earlier, later):
    return (earlier[0] * later[0], later[0][:, None, None] * earlier[1] + later[1])


MESH = pl.DeviceIdType.MESH


def fused_kernel(
    count, blocks, q_ref, k_ref, v_ref, noise_hbm, power_hbm, gain_hbm, out_ref,
    noise_ref, power_ref, gain_ref, small_done,
    q_all, k_all, v_all, outcome, fresh_mine, fresh_got,
    in_send, in_recv, out_send, out_recv, fresh_send, fresh_recv,
    ready, column_ready, all_ready,
):
    rows = q_ref.shape[0]
    depth = gain_ref.shape[1]
    grouped = q_all.shape[0]
    total_rows = count * rows
    factor = depth ** (-0.5)
    me, now = lax.axis_index("space"), lax.axis_index("tm")
    chips, half = count // 2, count // 4
    chip, core = me // 2, me % 2

    def place(device):
        return device + 1 - 2 * (device % 2)

    rank = place(me)

    def at_space(device):
        return {"device_id": {"space": device}, "device_id_type": MESH}

    def at_tm(step):
        return {"device_id": {"tm": lax.rem(now + step, blocks)}, "device_id_type": MESH}

    low = chip < half
    targets = []
    for k in range(chips):
        if k == 0:
            below = chip
        elif k < half:
            below = k - 1 + jnp.where(k - 1 >= chip, 1, 0)
        else:
            below = k
        if k < half:
            above = half - 1 - k
        elif k == half:
            above = chip
        else:
            above = k - 1 + jnp.where(k - 1 >= chip, 1, 0)
        there = jnp.where(low, below, above)
        targets.append((there, 2 * there + core, 2 * there + 1 - core))

    small = [
        pltpu.make_async_copy(held, here, small_done.at[index])
        for index, (held, here) in enumerate(
            ((noise_hbm, noise_ref), (power_hbm, power_ref), (gain_hbm, gain_ref))
        )
    ]

    barrier = pltpu.get_barrier_semaphore()
    is_hub = rank == 0
    for other in range(count - 1, -1, -1):

        @pl.when(place(other) > rank)
        def _():
            pl.semaphore_signal(barrier, inc=1, **at_space(other))

    @pl.when(is_hub)
    def _():
        for step in range(1, blocks):
            pl.semaphore_signal(barrier, inc=1, **at_tm(step))

    for copy in small:
        copy.start()
    pl.semaphore_wait(barrier, jnp.where(is_hub, blocks - 1, rank))
    for other in range(count):

        @pl.when(place(other) < rank)
        def _():
            pl.semaphore_signal(ready.at[me], inc=1, **at_space(other))

    def lanes(head):
        return pl.ds(pl.multiple_of(head * depth, depth), depth)

    def part(device):
        return pl.ds(pl.multiple_of(device * rows, rows), rows)

    arrays = ((k_ref, k_all), (v_ref, v_all), (q_ref, q_all))

    def send_input(device, slot, which):
        if slot == 0 and which == 0:

            @pl.when(place(device) > rank)
            def _():
                pl.semaphore_wait(ready.at[device], 1)

        source, target = arrays[which]
        pltpu.make_async_remote_copy(
            src_ref=source.at[:, lanes(device * grouped + slot)],
            dst_ref=target.at[slot, part(me)],
            send_sem=in_send.at[slot, which],
            recv_sem=in_recv.at[slot, which],
            **at_space(device),
        ).start()

    for slot in range(grouped):
        for which in range(len(arrays)):
            for there, same, opposite in targets:

                @pl.when(there != chip)
                def _():
                    send_input(same, slot, which)

                send_input(opposite, slot, which)

    for slot in range(grouped):
        for which, (source, target) in enumerate(arrays):
            pltpu.make_async_copy(
                source.at[:, lanes(me * grouped + slot)],
                target.at[slot, part(me)],
                in_recv.at[slot, which],
            ).start()

    @pl.when(is_hub)
    def _():
        for step in range(1, blocks):
            pl.semaphore_signal(column_ready, inc=1, **at_tm(step))
        pl.semaphore_wait(column_ready, blocks - 1)
        for other in range(count):
            if place(other) > 0:
                pl.semaphore_signal(all_ready, inc=1, **at_space(other))

    @pl.when(rank > 0)
    def _():
        pl.semaphore_wait(all_ready, 1)

    def arrived(slot, which):
        whole = arrays[which][1].at[slot]
        pltpu.make_async_copy(whole, whole, in_recv.at[slot, which]).wait()

    def give_back(slot, device):
        pltpu.make_async_remote_copy(
            src_ref=outcome.at[slot, part(device)],
            dst_ref=out_ref.at[:, lanes(me * grouped + slot)],
            send_sem=out_send.at[slot],
            recv_sem=out_recv.at[0],
            **at_space(device),
        ).start()

    far_chips = [half * jnp.where(low, 1, 0) + k for k in range(half)]
    near_chips = [half * jnp.where(low, 0, 1) + k for k in range(half)]

    def give_far(slot):
        for there in far_chips:
            for digit in range(2):
                give_back(slot, 2 * there + digit)

    def give_near(slot):
        for there in near_chips:

            @pl.when(there != chip)
            def _():
                give_back(slot, 2 * there)
                give_back(slot, 2 * there + 1)

        give_back(slot, 2 * chip + 1 - core)

    for copy in small:
        copy.wait()
    level = jnp.full((8, depth), noise_ref[0], jnp.int32).astype(jnp.float32)
    for slot in range(grouped):
        head = me * grouped + slot
        power = jnp.full((8, depth), power_ref[head], jnp.int32).astype(jnp.float32)
        rate = jnp.exp2(-(power * (0.25 + 1.75 * level / LEVELS)) / blocks)
        arrived(slot, 0)
        arrived(slot, 1)
        fresh = lax.dot_general(
            k_all[slot], v_all[slot], (((0,), (0,)), ((), ())), preferred_element_type=jnp.float32
        )
        fresh_mine[slot, 0:depth, :] = fresh / total_rows
        fresh_mine[slot, depth : depth + 8, :] = rate
        for step in range(1, blocks):
            pltpu.make_async_remote_copy(
                src_ref=fresh_mine.at[slot],
                dst_ref=fresh_got.at[slot, step - 1],
                send_sem=fresh_send.at[slot],
                recv_sem=fresh_recv.at[slot],
                **at_tm(step),
            ).start()
        arrived(slot, 2)
        landed = fresh_got.at[slot]
        pltpu.make_async_copy(landed, landed, fresh_recv.at[slot]).wait()
        carried = jnp.zeros((depth, depth), jnp.float32)
        for step in range(blocks - 1, 0, -1):
            longer = (
                fresh_got[slot, step - 1, depth : depth + 1, :] * carried
                + fresh_got[slot, step - 1, 0:depth, :]
            )
            carried = jnp.where(now - step >= 0, longer, carried)
        state = (rate[0:1, :] * carried).astype(jnp.bfloat16)
        gain_row = gain_ref[pl.ds(head, 1), :]

        def attend(first_chip):
            span = pl.ds(pl.multiple_of(first_chip * 2 * rows, 2 * half * rows), 2 * half * rows)
            query = q_all[slot, span, :]
            scores = lax.dot_general(
                query, k_all[slot], (((1,), (1,)), ((), ())), preferred_element_type=jnp.float32
            ) * factor
            weights = jnp.exp(scores - jnp.max(scores, axis=1, keepdims=True))
            row_total = jnp.sum(weights, axis=1, keepdims=True)
            numerator = jnp.dot(
                weights.astype(jnp.bfloat16), v_all[slot], preferred_element_type=jnp.float32
            )
            before = jnp.dot(query, state, preferred_element_type=jnp.float32) * factor
            mixed = numerator / row_total + before
            scale = lax.rsqrt(jnp.mean(mixed * mixed, axis=1, keepdims=True) + epsilon)
            outcome[slot, span, :] = (mixed * scale * gain_row).astype(jnp.bfloat16)

        attend(far_chips[0])
        if slot == grouped - 1:
            give_far(slot)
        attend(near_chips[0])
        give_near(slot)
        if slot == grouped - 2:
            for earlier in range(slot + 1):
                give_far(earlier)
        pltpu.make_async_copy(
            outcome.at[slot, part(me)], out_ref.at[:, lanes(head)], out_recv.at[0]
        ).start()

    for slot in range(grouped):
        for which in range(len(arrays)):
            sent = arrays[which][1].at[slot, pl.ds(0, total_rows - rows)]
            pltpu.make_async_copy(sent, sent, in_send.at[slot, which]).wait()
        landed = fresh_got.at[slot]
        pltpu.make_async_copy(landed, landed, fresh_send.at[slot]).wait()
        returned = outcome.at[slot, pl.ds(0, total_rows - rows)]
        pltpu.make_async_copy(returned, returned, out_send.at[slot]).wait()
    pltpu.make_async_copy(out_ref, out_ref, out_recv.at[0]).wait()


def fused(queries, key_rows, value_rows, noise_level, decay_power, head_gain):
    count, blocks = lax.axis_size("space"), lax.axis_size("tm")
    rows, width = queries.shape[1:]
    heads_total, depth = head_gain.shape
    grouped = heads_total // count
    held = [
        pltpu.with_memory_space_constraint(operand, pltpu.HBM)
        for operand in (queries[0], key_rows[0], value_rows[0], decay_power, head_gain)
    ]
    held.insert(3, noise_level)
    gathered = pltpu.VMEM((grouped, count * rows, depth), jnp.bfloat16)
    dma = pltpu.SemaphoreType.DMA
    out = pl.pallas_call(
        functools.partial(fused_kernel, count, blocks),
        out_shape=jax.ShapeDtypeStruct((rows, width), jnp.bfloat16),
        in_specs=[pl.BlockSpec(memory_space=pl.ANY)] * len(held),
        out_specs=pl.BlockSpec(memory_space=pl.ANY),
        scratch_shapes=[
            pltpu.SMEM(noise_level.shape, jnp.int32),
            pltpu.SMEM(decay_power.shape, jnp.int32),
            pltpu.VMEM(head_gain.shape, jnp.float32),
            dma((3,)),
            gathered,
            gathered,
            gathered,
            gathered,
            pltpu.VMEM((grouped, depth + 8, depth), jnp.float32),
            pltpu.VMEM((grouped, blocks - 1, depth + 8, depth), jnp.float32),
            dma((grouped, 3)),
            dma((grouped, 3)),
            dma((grouped,)),
            dma((1,)),
            dma((grouped,)),
            dma((grouped,)),
            pltpu.SemaphoreType.REGULAR((count,)),
            pltpu.SemaphoreType.REGULAR,
            pltpu.SemaphoreType.REGULAR,
        ],
        compiler_params=pltpu.CompilerParams(collective_id=0, has_side_effects=True, vmem_limit_bytes=VMEM_GRANT),
        name="heads_exchange",
    )(*held)
    return out[None]


def body(queries, key_rows, value_rows, noise_level, decay_power, head_gain):
    heads_total = decay_power.shape[0]
    depth = head_gain.shape[1]
    local_rows = queries.shape[1]
    quarters = lax.axis_size("space") // HGROUPS
    grouped = heads_total // HGROUPS
    query_items = spread_items(queries[0], quarters, heads_total, depth)
    keys_sent = copied_items(key_rows[0], quarters, heads_total, depth)
    values_sent = copied_items(value_rows[0], quarters, heads_total, depth)
    query_got, keys_got, values_got = (
        lax.all_to_all(query_items, "space", split_axis=0, concat_axis=1, tiled=True),
        lax.all_to_all(keys_sent, "space", split_axis=0, concat_axis=1, tiled=True),
        lax.all_to_all(values_sent, "space", split_axis=0, concat_axis=1, tiled=True),
    )
    key_count = keys_got.shape[1]
    fresh = (
        jnp.einsum("inh,ine->ihe", keys_got, values_got, preferred_element_type=jnp.float32)
        / key_count
    )
    group_index = lax.axis_index("space") % HGROUPS
    powers = lax.dynamic_slice_in_dim(decay_power, group_index * grouped, grouped).astype(
        jnp.float32
    )
    level_now = noise_level[0].astype(jnp.float32)
    block_count = lax.axis_size("tm")
    rate = jnp.exp2(-(powers * (0.25 + 1.75 * level_now / LEVELS)) / block_count)
    zeros_state = jnp.zeros_like(fresh)
    unused_rate, before = carried_in(
        (rate, fresh), "tm", compose, (jnp.ones_like(rate), zeros_state)
    )
    state = (rate[:, None, None] * before).astype(jnp.bfloat16)
    gain_rows = lax.dynamic_slice_in_dim(head_gain, group_index * grouped, grouped)
    outcome = lax.map(attend_head, (query_got, keys_got, values_got, state, gain_rows))
    returned = lax.all_to_all(outcome, "space", split_axis=1, concat_axis=0, tiled=True)
    part_rows = local_rows // quarters
    restored = returned.reshape(quarters, heads_total, part_rows, depth).transpose(0, 2, 1, 3)
    return restored.reshape(1, local_rows, heads_total * depth)


def solution(mesh):
    in_specs = (
        P("tm", "space", None),
        P("tm", "space", None),
        P("tm", "space", None),
        P("tm"),
        P(),
        P(),
    )
    out_specs = P("tm", "space", None)
    step = fused if mesh.shape["space"] == HGROUPS else body
    return jax.shard_map(step, mesh=mesh, in_specs=in_specs, out_specs=out_specs, check_vma=False)
```

```python
import functools

import jax
import jax.numpy as jnp
from jax import lax
from jax.experimental import pallas as pl
from jax.experimental.pallas import tpu as pltpu
from jax.sharding import PartitionSpec as P

LEVELS = 1000
HGROUPS = 8
VMEM_GRANT = 32 * 2**20


epsilon = 1e-06


def carried_in(value, axis, join, neutral):
    count, mine = (lax.axis_size(axis), lax.axis_index(axis))
    pieces = jax.tree.map(lambda part: lax.all_gather(part, axis), value)
    so_far = jax.tree.map(
        lambda part, zero: jnp.full_like(part, 0) + jnp.asarray(zero, part.dtype), value, neutral
    )

    def lap(position, so_far):
        longer = join(so_far, jax.tree.map(lambda part: part[position], pieces))
        return jax.tree.map(lambda new, old: jnp.where(position < mine, new, old), longer, so_far)

    return lax.fori_loop(0, count - 1, lap, so_far)


def spread_items(block, quarters, heads_total, depth):
    part_rows = block.shape[0] // quarters
    shaped = block.reshape(quarters, part_rows, heads_total, depth).transpose(0, 2, 1, 3)
    return shaped.reshape(quarters * heads_total, part_rows, depth)


def copied_items(block, quarters, heads_total, depth):
    every = block.reshape(block.shape[0], heads_total, depth).transpose(1, 0, 2)
    copied = jnp.broadcast_to(every[None], (quarters,) + every.shape)
    return copied.reshape(quarters * heads_total, block.shape[0], depth)


def attend_head(bundle):
    query, key_item, value_item, state, gain_row = bundle
    factor = query.shape[1] ** (-0.5)
    scores = jnp.dot(query, key_item.T, preferred_element_type=jnp.float32) * factor
    row_top = jnp.max(scores, axis=1, keepdims=True)
    weights = jnp.exp(scores - row_top)
    row_total = jnp.sum(weights, axis=1, keepdims=True)
    numerator = jnp.dot(
        weights.astype(jnp.bfloat16), value_item, preferred_element_type=jnp.float32
    )
    carried = jnp.dot(query, state, preferred_element_type=jnp.float32) * factor
    mixed = numerator / row_total + carried
    normed = mixed * lax.rsqrt(jnp.mean(mixed * mixed, axis=1, keepdims=True) + epsilon) * gain_row
    return normed.astype(jnp.bfloat16)


def compose(earlier, later):
    return (earlier[0] * later[0], later[0][:, None, None] * earlier[1] + later[1])


MESH = pl.DeviceIdType.MESH


def fused_kernel(
    count, blocks, q_ref, k_ref, v_ref, noise_hbm, power_hbm, gain_hbm, out_ref,
    noise_ref, power_ref, gain_ref, small_done,
    q_all, k_all, v_all, outcome, fresh_mine, fresh_got,
    in_send, in_recv, out_send, out_recv, fresh_send, fresh_recv,
    first_send, ready, column_ready, all_ready,
):
    rows = q_ref.shape[0]
    depth = gain_ref.shape[1]
    grouped = q_all.shape[0]
    total_rows = count * rows
    factor = depth ** (-0.5)
    me, now = lax.axis_index("space"), lax.axis_index("tm")
    chips, half = count // 2, count // 4
    chip, core = me // 2, me % 2

    def place(device):
        return device + 1 - 2 * (device % 2)

    rank = place(me)

    def at_space(device):
        return {"device_id": {"space": device}, "device_id_type": MESH}

    def at_tm(step):
        return {"device_id": {"tm": lax.rem(now + step, blocks)}, "device_id_type": MESH}

    low = chip < half
    targets = []
    for k in range(chips):
        if True:
            if k == 0:
                below = chip
            elif k < half:
                below = k - 1 + jnp.where(k - 1 >= chip, 1, 0)
            else:
                below = k
        else:
            if k < half:
                below = half + k
            elif k == half:
                below = chip
            else:
                below = k - half - 1 + jnp.where(k - half - 1 >= chip, 1, 0)
        if k < half:
            above = half - 1 - k
        elif k == half:
            above = chip
        else:
            above = k - 1 + jnp.where(k - 1 >= chip, 1, 0)
        there = jnp.where(low, below, above)
        targets.append((there, 2 * there + core, 2 * there + 1 - core))

    small = [
        pltpu.make_async_copy(held, here, small_done.at[index])
        for index, (held, here) in enumerate(
            ((noise_hbm, noise_ref), (power_hbm, power_ref), (gain_hbm, gain_ref))
        )
    ]

    barrier = pltpu.get_barrier_semaphore()
    is_hub = rank == 0
    for other in range(count - 1, -1, -1):

        @pl.when(place(other) > rank)
        def _():
            pl.semaphore_signal(barrier, inc=1, **at_space(other))

    @pl.when(is_hub)
    def _():
        for step in range(1, blocks):
            pl.semaphore_signal(barrier, inc=1, **at_tm(step))

    for copy in small:
        copy.start()
    pl.semaphore_wait(barrier, jnp.where(is_hub, blocks - 1, rank))
    for other in range(count):

        @pl.when(place(other) < rank)
        def _():
            pl.semaphore_signal(ready.at[me], inc=1, **at_space(other))

    def lanes(head):
        return pl.ds(pl.multiple_of(head * depth, depth), depth)

    def part(device):
        return pl.ds(pl.multiple_of(device * rows, rows), rows)

    arrays = ((k_ref, k_all), (v_ref, v_all), (q_ref, q_all))

    def send_input(device, slot, which):
        if slot == 0 and which == 0:

            @pl.when(place(device) > rank)
            def _():
                pl.semaphore_wait(ready.at[device], 1)

        source, target = arrays[which]
        pltpu.make_async_remote_copy(
            src_ref=source.at[:, lanes(device * grouped + slot)],
            dst_ref=target.at[slot, part(me)],
            send_sem=in_send.at[slot, which],
            recv_sem=in_recv.at[slot, which],
            **at_space(device),
        ).start()

    for slot in range(grouped):
        for which in range(len(arrays)):
            for there, same, opposite in targets:

                @pl.when(there != chip)
                def _():
                    send_input(same, slot, which)

                send_input(opposite, slot, which)

    for slot in range(grouped):
        for which, (source, target) in enumerate(arrays):
            pltpu.make_async_copy(
                source.at[:, lanes(me * grouped + slot)],
                target.at[slot, part(me)],
                in_recv.at[slot, which],
            ).start()

    @pl.when(is_hub)
    def _():
        for step in range(1, blocks):
            pl.semaphore_signal(column_ready, inc=1, **at_tm(step))
        pl.semaphore_wait(column_ready, blocks - 1)
        for other in range(count):
            if place(other) > 0:
                pl.semaphore_signal(all_ready, inc=1, **at_space(other))

    @pl.when(rank > 0)
    def _():
        pl.semaphore_wait(all_ready, 1)

    def arrived(slot, which):
        whole = arrays[which][1].at[slot]
        pltpu.make_async_copy(whole, whole, in_recv.at[slot, which]).wait()

    def give_back(slot, device, done=None):
        pltpu.make_async_remote_copy(
            src_ref=outcome.at[slot, part(device)],
            dst_ref=out_ref.at[:, lanes(me * grouped + slot)],
            send_sem=out_send.at[slot] if done is None else done,
            recv_sem=out_recv.at[0],
            **at_space(device),
        ).start()

    far_chips = [jnp.where(low, half + k, k) for k in range(half)]
    near_chips = [half * jnp.where(low, 0, 1) + k for k in range(half)]

    def give_far(slot, which):
        for digit in range(2):
            give_back(
                slot, 2 * far_chips[which] + digit,
                first_send.at[slot // (grouped - 1)] if which == 0 else None,
            )

    def give_near(slot):
        for there in near_chips:

            @pl.when(there != chip)
            def _():
                give_back(slot, 2 * there)
                give_back(slot, 2 * there + 1)

        give_back(slot, 2 * chip + 1 - core)

    for copy in small:
        copy.wait()
    level = jnp.full((8, depth), noise_ref[0], jnp.int32).astype(jnp.float32)
    for slot in range(grouped):
        head = me * grouped + slot
        power = jnp.full((8, depth), power_ref[head], jnp.int32).astype(jnp.float32)
        rate = jnp.exp2(-(power * (0.25 + 1.75 * level / LEVELS)) / blocks)
        arrived(slot, 0)
        arrived(slot, 1)
        fresh = lax.dot_general(
            k_all[slot], v_all[slot], (((0,), (0,)), ((), ())), preferred_element_type=jnp.float32
        )
        fresh_mine[slot, 0:depth, :] = fresh / total_rows
        fresh_mine[slot, depth : depth + 8, :] = rate
        for step in range(1, blocks):
            pltpu.make_async_remote_copy(
                src_ref=fresh_mine.at[slot],
                dst_ref=fresh_got.at[slot, step - 1],
                send_sem=fresh_send.at[slot],
                recv_sem=fresh_recv.at[slot],
                **at_tm(step),
            ).start()
        arrived(slot, 2)
        landed = fresh_got.at[slot]
        pltpu.make_async_copy(landed, landed, fresh_recv.at[slot]).wait()
        carried = jnp.zeros((depth, depth), jnp.float32)
        for step in range(blocks - 1, 0, -1):
            longer = (
                fresh_got[slot, step - 1, depth : depth + 1, :] * carried
                + fresh_got[slot, step - 1, 0:depth, :]
            )
            carried = jnp.where(now - step >= 0, longer, carried)
        state = (rate[0:1, :] * carried).astype(jnp.bfloat16)
        gain_row = gain_ref[pl.ds(head, 1), :]

        def attend(first_chip):
            span = pl.ds(pl.multiple_of(first_chip * 2 * rows, 2 * half * rows), 2 * half * rows)
            query = q_all[slot, span, :]
            scores = lax.dot_general(
                query, k_all[slot], (((1,), (1,)), ((), ())), preferred_element_type=jnp.float32
            ) * factor
            weights = jnp.exp(scores - jnp.max(scores, axis=1, keepdims=True))
            row_total = jnp.sum(weights, axis=1, keepdims=True)
            numerator = jnp.dot(
                weights.astype(jnp.bfloat16), v_all[slot], preferred_element_type=jnp.float32
            )
            before = jnp.dot(query, state, preferred_element_type=jnp.float32) * factor
            mixed = numerator / row_total + before
            scale = lax.rsqrt(jnp.mean(mixed * mixed, axis=1, keepdims=True) + epsilon)
            outcome[slot, span, :] = (mixed * scale * gain_row).astype(jnp.bfloat16)

        attend(half * jnp.where(low, 1, 0))
        if slot == grouped - 1:
            give_far(slot, 0)
        attend(near_chips[0])
        give_near(slot)
        if slot == grouped - 2:
            for earlier in range(grouped - 1):
                give_far(earlier, 0)
            for earlier in range(2):
                give_far(earlier, 1)
        if slot == grouped - 1:
            @pl.when(jnp.logical_not(low))
            def _():
                first = outcome.at[0, pl.ds(0, 2 * rows * (grouped - 1))]
                pltpu.make_async_copy(first, first, first_send.at[0]).wait()

            for earlier in range(2, grouped):
                give_far(earlier, 1)
        pltpu.make_async_copy(
            outcome.at[slot, part(me)], out_ref.at[:, lanes(head)], out_recv.at[0]
        ).start()

    @pl.when(low)
    def _():
        first = outcome.at[0, pl.ds(0, 2 * rows * (grouped - 1))]
        pltpu.make_async_copy(first, first, first_send.at[0]).wait()

    last = outcome.at[0, pl.ds(0, 2 * rows)]
    pltpu.make_async_copy(last, last, first_send.at[1]).wait()
    for slot in range(grouped):
        for which in range(len(arrays)):
            sent = arrays[which][1].at[slot, pl.ds(0, total_rows - rows)]
            pltpu.make_async_copy(sent, sent, in_send.at[slot, which]).wait()
        landed = fresh_got.at[slot]
        pltpu.make_async_copy(landed, landed, fresh_send.at[slot]).wait()
        returned = outcome.at[slot, pl.ds(0, total_rows - 3 * rows)]
        pltpu.make_async_copy(returned, returned, out_send.at[slot]).wait()
    pltpu.make_async_copy(out_ref, out_ref, out_recv.at[0]).wait()


def fused(queries, key_rows, value_rows, noise_level, decay_power, head_gain):
    count, blocks = lax.axis_size("space"), lax.axis_size("tm")
    rows, width = queries.shape[1:]
    heads_total, depth = head_gain.shape
    grouped = heads_total // count
    held = [
        pltpu.with_memory_space_constraint(operand, pltpu.HBM)
        for operand in (queries[0], key_rows[0], value_rows[0], decay_power, head_gain)
    ]
    held.insert(3, noise_level)
    gathered = pltpu.VMEM((grouped, count * rows, depth), jnp.bfloat16)
    dma = pltpu.SemaphoreType.DMA
    out = pl.pallas_call(
        functools.partial(fused_kernel, count, blocks),
        out_shape=jax.ShapeDtypeStruct((rows, width), jnp.bfloat16),
        in_specs=[pl.BlockSpec(memory_space=pl.ANY)] * len(held),
        out_specs=pl.BlockSpec(memory_space=pl.ANY),
        scratch_shapes=[
            pltpu.SMEM(noise_level.shape, jnp.int32),
            pltpu.SMEM(decay_power.shape, jnp.int32),
            pltpu.VMEM(head_gain.shape, jnp.float32),
            dma((3,)),
            gathered,
            gathered,
            gathered,
            gathered,
            pltpu.VMEM((grouped, depth + 8, depth), jnp.float32),
            pltpu.VMEM((grouped, blocks - 1, depth + 8, depth), jnp.float32),
            dma((grouped, 3)),
            dma((grouped, 3)),
            dma((grouped,)),
            dma((1,)),
            dma((grouped,)),
            dma((grouped,)),
            dma((2,)),
            pltpu.SemaphoreType.REGULAR((count,)),
            pltpu.SemaphoreType.REGULAR,
            pltpu.SemaphoreType.REGULAR,
        ],
        compiler_params=pltpu.CompilerParams(collective_id=0, has_side_effects=True, vmem_limit_bytes=VMEM_GRANT),
        name="heads_exchange",
    )(*held)
    return out[None]


def body(queries, key_rows, value_rows, noise_level, decay_power, head_gain):
    heads_total = decay_power.shape[0]
    depth = head_gain.shape[1]
    local_rows = queries.shape[1]
    quarters = lax.axis_size("space") // HGROUPS
    grouped = heads_total // HGROUPS
    query_items = spread_items(queries[0], quarters, heads_total, depth)
    keys_sent = copied_items(key_rows[0], quarters, heads_total, depth)
    values_sent = copied_items(value_rows[0], quarters, heads_total, depth)
    query_got, keys_got, values_got = (
        lax.all_to_all(query_items, "space", split_axis=0, concat_axis=1, tiled=True),
        lax.all_to_all(keys_sent, "space", split_axis=0, concat_axis=1, tiled=True),
        lax.all_to_all(values_sent, "space", split_axis=0, concat_axis=1, tiled=True),
    )
    key_count = keys_got.shape[1]
    fresh = (
        jnp.einsum("inh,ine->ihe", keys_got, values_got, preferred_element_type=jnp.float32)
        / key_count
    )
    group_index = lax.axis_index("space") % HGROUPS
    powers = lax.dynamic_slice_in_dim(decay_power, group_index * grouped, grouped).astype(
        jnp.float32
    )
    level_now = noise_level[0].astype(jnp.float32)
    block_count = lax.axis_size("tm")
    rate = jnp.exp2(-(powers * (0.25 + 1.75 * level_now / LEVELS)) / block_count)
    zeros_state = jnp.zeros_like(fresh)
    unused_rate, before = carried_in(
        (rate, fresh), "tm", compose, (jnp.ones_like(rate), zeros_state)
    )
    state = (rate[:, None, None] * before).astype(jnp.bfloat16)
    gain_rows = lax.dynamic_slice_in_dim(head_gain, group_index * grouped, grouped)
    outcome = lax.map(attend_head, (query_got, keys_got, values_got, state, gain_rows))
    returned = lax.all_to_all(outcome, "space", split_axis=1, concat_axis=0, tiled=True)
    part_rows = local_rows // quarters
    restored = returned.reshape(quarters, heads_total, part_rows, depth).transpose(0, 2, 1, 3)
    return restored.reshape(1, local_rows, heads_total * depth)


def solution(mesh):
    in_specs = (
        P("tm", "space", None),
        P("tm", "space", None),
        P("tm", "space", None),
        P("tm"),
        P(),
        P(),
    )
    out_specs = P("tm", "space", None)
    step = fused if mesh.shape["space"] == HGROUPS else body
    return jax.shard_map(step, mesh=mesh, in_specs=in_specs, out_specs=out_specs, check_vma=False)
```

```python
import functools

import jax
import jax.numpy as jnp
from jax import lax
from jax.experimental import pallas as pl
from jax.experimental.pallas import tpu as pltpu
from jax.sharding import PartitionSpec as P

LEVELS = 1000
HGROUPS = 8
VMEM_GRANT = 32 * 2**20


epsilon = 1e-06


def carried_in(value, axis, join, neutral):
    count, mine = (lax.axis_size(axis), lax.axis_index(axis))
    pieces = jax.tree.map(lambda part: lax.all_gather(part, axis), value)
    so_far = jax.tree.map(
        lambda part, zero: jnp.full_like(part, 0) + jnp.asarray(zero, part.dtype), value, neutral
    )

    def lap(position, so_far):
        longer = join(so_far, jax.tree.map(lambda part: part[position], pieces))
        return jax.tree.map(lambda new, old: jnp.where(position < mine, new, old), longer, so_far)

    return lax.fori_loop(0, count - 1, lap, so_far)


def spread_items(block, quarters, heads_total, depth):
    part_rows = block.shape[0] // quarters
    shaped = block.reshape(quarters, part_rows, heads_total, depth).transpose(0, 2, 1, 3)
    return shaped.reshape(quarters * heads_total, part_rows, depth)


def copied_items(block, quarters, heads_total, depth):
    every = block.reshape(block.shape[0], heads_total, depth).transpose(1, 0, 2)
    copied = jnp.broadcast_to(every[None], (quarters,) + every.shape)
    return copied.reshape(quarters * heads_total, block.shape[0], depth)


def attend_head(bundle):
    query, key_item, value_item, state, gain_row = bundle
    factor = query.shape[1] ** (-0.5)
    scores = jnp.dot(query, key_item.T, preferred_element_type=jnp.float32) * factor
    row_top = jnp.max(scores, axis=1, keepdims=True)
    weights = jnp.exp(scores - row_top)
    row_total = jnp.sum(weights, axis=1, keepdims=True)
    numerator = jnp.dot(
        weights.astype(jnp.bfloat16), value_item, preferred_element_type=jnp.float32
    )
    carried = jnp.dot(query, state, preferred_element_type=jnp.float32) * factor
    mixed = numerator / row_total + carried
    normed = mixed * lax.rsqrt(jnp.mean(mixed * mixed, axis=1, keepdims=True) + epsilon) * gain_row
    return normed.astype(jnp.bfloat16)


def compose(earlier, later):
    return (earlier[0] * later[0], later[0][:, None, None] * earlier[1] + later[1])


MESH = pl.DeviceIdType.MESH


def fused_kernel(
    count, blocks, q_ref, k_ref, v_ref, noise_hbm, power_hbm, gain_hbm, out_ref,
    noise_ref, power_ref, gain_ref, small_done,
    q_all, k_all, v_all, outcome, fresh_mine, fresh_got,
    in_send, in_recv, out_send, out_recv, fresh_send, fresh_recv,
    first_send, ready, column_ready, all_ready,
):
    rows = q_ref.shape[0]
    depth = gain_ref.shape[1]
    grouped = q_all.shape[0]
    total_rows = count * rows
    factor = depth ** (-0.5)
    me, now = lax.axis_index("space"), lax.axis_index("tm")
    chips, half = count // 2, count // 4
    chip, core = me // 2, me % 2

    def place(device):
        return device + 1 - 2 * (device % 2)

    rank = place(me)

    def at_space(device):
        return {"device_id": {"space": device}, "device_id_type": MESH}

    def at_tm(step):
        return {"device_id": {"tm": lax.rem(now + step, blocks)}, "device_id_type": MESH}

    low = chip < half
    targets = []
    for k in range(chips):
        if True:
            if k == 0:
                below = chip
            elif k < half:
                below = k - 1 + jnp.where(k - 1 >= chip, 1, 0)
            else:
                below = k
        else:
            if k < half:
                below = half + k
            elif k == half:
                below = chip
            else:
                below = k - half - 1 + jnp.where(k - half - 1 >= chip, 1, 0)
        if k < half:
            above = half - 1 - k
        else:
            above = k
        there = jnp.where(low, below, above)
        targets.append((there, 2 * there + core, 2 * there + 1 - core))

    small = [
        pltpu.make_async_copy(held, here, small_done.at[index])
        for index, (held, here) in enumerate(
            ((noise_hbm, noise_ref), (power_hbm, power_ref), (gain_hbm, gain_ref))
        )
    ]

    barrier = pltpu.get_barrier_semaphore()
    is_hub = rank == 0
    is_last = chip == chips - 1
    for other in range(count - 1, -1, -1):

        @pl.when(jnp.logical_and(me != other, jnp.logical_or(jnp.logical_not(is_last), place(other) > rank)))
        def _():
            pl.semaphore_signal(barrier, inc=1, **at_space(other))

    @pl.when(is_hub)
    def _():
        for step in range(1, blocks):
            pl.semaphore_signal(barrier, inc=1, **at_tm(step))

    pl.semaphore_wait(
        barrier, jnp.where(is_last, rank, count - 3 + jnp.where(is_hub, blocks - 1, 0))
    )

    @pl.when(is_last)
    def _():
        for other in range(count):

            @pl.when(place(other) < rank)
            def _():
                pl.semaphore_signal(ready.at[me], inc=1, **at_space(other))

    def lanes(head):
        return pl.ds(pl.multiple_of(head * depth, depth), depth)

    def part(device):
        return pl.ds(pl.multiple_of(device * rows, rows), rows)

    arrays = ((k_ref, k_all), (v_ref, v_all), (q_ref, q_all))

    def send_input(device, slot, which):
        source, target = arrays[which]
        pltpu.make_async_remote_copy(
            src_ref=source.at[:, lanes(device * grouped + slot)],
            dst_ref=target.at[slot, part(me)],
            send_sem=in_send.at[slot, which],
            recv_sem=in_recv.at[slot, which],
            **at_space(device),
        ).start()

    def send_chip(position, slot, which):
        there, same, opposite = targets[position]

        @pl.when(there != chip)
        def _():
            send_input(same, slot, which)

        send_input(opposite, slot, which)

    for slot in range(grouped):
        known = chips - 1 if slot == 0 else chips
        for which in range(len(arrays)):
            for position in range(known):
                send_chip(position, slot, which)
        if slot == 0:
            for device in (count - 2, count - 1):

                @pl.when(place(device) > rank)
                def _():
                    pl.semaphore_wait(ready.at[device], 1)

            for which in range(len(arrays)):
                send_chip(chips - 1, slot, which)

    for slot in range(grouped):
        for which, (source, target) in enumerate(arrays):
            pltpu.make_async_copy(
                source.at[:, lanes(me * grouped + slot)],
                target.at[slot, part(me)],
                in_recv.at[slot, which],
            ).start()

    for copy in small:
        copy.start()

    @pl.when(is_hub)
    def _():
        for step in range(1, blocks):
            pl.semaphore_signal(column_ready, inc=1, **at_tm(step))
        pl.semaphore_wait(column_ready, blocks - 1)
        for other in range(count):
            if place(other) > 0:
                pl.semaphore_signal(all_ready, inc=1, **at_space(other))

    @pl.when(rank > 0)
    def _():
        pl.semaphore_wait(all_ready, 1)

    def arrived(slot, which):
        whole = arrays[which][1].at[slot]
        pltpu.make_async_copy(whole, whole, in_recv.at[slot, which]).wait()

    def give_back(slot, device, done=None):
        pltpu.make_async_remote_copy(
            src_ref=outcome.at[slot, part(device)],
            dst_ref=out_ref.at[:, lanes(me * grouped + slot)],
            send_sem=out_send.at[slot] if done is None else done,
            recv_sem=out_recv.at[0],
            **at_space(device),
        ).start()

    far_chips = [jnp.where(low, half + k, k) for k in range(half)]
    near_chips = [half * jnp.where(low, 0, 1) + k for k in range(half)]

    def give_far(slot, which):
        for digit in range(2):
            give_back(
                slot, 2 * far_chips[which] + digit,
                first_send.at[slot // (grouped - 1)] if which == 0 else None,
            )

    def give_near(slot):
        for there in near_chips:

            @pl.when(there != chip)
            def _():
                give_back(slot, 2 * there)
                give_back(slot, 2 * there + 1)

        give_back(slot, 2 * chip + 1 - core)

    for copy in small:
        copy.wait()
    level = jnp.full((8, depth), noise_ref[0], jnp.int32).astype(jnp.float32)
    for slot in range(grouped):
        head = me * grouped + slot
        power = jnp.full((8, depth), power_ref[head], jnp.int32).astype(jnp.float32)
        rate = jnp.exp2(-(power * (0.25 + 1.75 * level / LEVELS)) / blocks)
        arrived(slot, 0)
        arrived(slot, 1)
        fresh = lax.dot_general(
            k_all[slot], v_all[slot], (((0,), (0,)), ((), ())), preferred_element_type=jnp.float32
        )
        fresh_mine[slot, 0:depth, :] = fresh / total_rows
        fresh_mine[slot, depth : depth + 8, :] = rate
        for step in range(1, blocks):
            pltpu.make_async_remote_copy(
                src_ref=fresh_mine.at[slot],
                dst_ref=fresh_got.at[slot, step - 1],
                send_sem=fresh_send.at[slot],
                recv_sem=fresh_recv.at[slot],
                **at_tm(step),
            ).start()
        arrived(slot, 2)
        landed = fresh_got.at[slot]
        pltpu.make_async_copy(landed, landed, fresh_recv.at[slot]).wait()
        carried = jnp.zeros((depth, depth), jnp.float32)
        for step in range(blocks - 1, 0, -1):
            longer = (
                fresh_got[slot, step - 1, depth : depth + 1, :] * carried
                + fresh_got[slot, step - 1, 0:depth, :]
            )
            carried = jnp.where(now - step >= 0, longer, carried)
        state = (rate[0:1, :] * carried).astype(jnp.bfloat16)
        gain_row = gain_ref[pl.ds(head, 1), :]

        def attend(first_chip):
            span = pl.ds(pl.multiple_of(first_chip * 2 * rows, 2 * half * rows), 2 * half * rows)
            query = q_all[slot, span, :]
            scores = lax.dot_general(
                query, k_all[slot], (((1,), (1,)), ((), ())), preferred_element_type=jnp.float32
            ) * factor
            weights = jnp.exp(scores - jnp.max(scores, axis=1, keepdims=True))
            row_total = jnp.sum(weights, axis=1, keepdims=True)
            numerator = jnp.dot(
                weights.astype(jnp.bfloat16), v_all[slot], preferred_element_type=jnp.float32
            )
            before = jnp.dot(query, state, preferred_element_type=jnp.float32) * factor
            mixed = numerator / row_total + before
            scale = lax.rsqrt(jnp.mean(mixed * mixed, axis=1, keepdims=True) + epsilon)
            outcome[slot, span, :] = (mixed * scale * gain_row).astype(jnp.bfloat16)

        attend(half * jnp.where(low, 1, 0))
        if slot == grouped - 1:
            give_far(slot, 0)
        attend(near_chips[0])
        give_near(slot)
        if slot == grouped - 2:
            for earlier in range(grouped - 1):
                give_far(earlier, 0)
            give_back(0, 2 * far_chips[1] + 0)
            give_back(0, 2 * far_chips[1] + 1)
            give_back(1, 2 * far_chips[1] + 0)
        if slot == grouped - 1:
            @pl.when(jnp.logical_not(low))
            def _():
                first = outcome.at[0, pl.ds(0, 2 * rows * (grouped - 1))]
                pltpu.make_async_copy(first, first, first_send.at[0]).wait()

            give_back(1, 2 * far_chips[1] + 1)
            give_back(2, 2 * far_chips[1] + 0)
            give_back(2, 2 * far_chips[1] + 1)
        pltpu.make_async_copy(
            outcome.at[slot, part(me)], out_ref.at[:, lanes(head)], out_recv.at[0]
        ).start()

    @pl.when(low)
    def _():
        first = outcome.at[0, pl.ds(0, 2 * rows * (grouped - 1))]
        pltpu.make_async_copy(first, first, first_send.at[0]).wait()

    last = outcome.at[0, pl.ds(0, 2 * rows)]
    pltpu.make_async_copy(last, last, first_send.at[1]).wait()
    for slot in range(grouped):
        for which in range(len(arrays)):
            sent = arrays[which][1].at[slot, pl.ds(0, total_rows - rows)]
            pltpu.make_async_copy(sent, sent, in_send.at[slot, which]).wait()
        landed = fresh_got.at[slot]
        pltpu.make_async_copy(landed, landed, fresh_send.at[slot]).wait()
        returned = outcome.at[slot, pl.ds(0, total_rows - 3 * rows)]
        pltpu.make_async_copy(returned, returned, out_send.at[slot]).wait()
    pltpu.make_async_copy(out_ref, out_ref, out_recv.at[0]).wait()


def fused(queries, key_rows, value_rows, noise_level, decay_power, head_gain):
    count, blocks = lax.axis_size("space"), lax.axis_size("tm")
    rows, width = queries.shape[1:]
    heads_total, depth = head_gain.shape
    grouped = heads_total // count
    held = [
        pltpu.with_memory_space_constraint(operand, pltpu.HBM)
        for operand in (queries[0], key_rows[0], value_rows[0], decay_power, head_gain)
    ]
    held.insert(3, noise_level)
    gathered = pltpu.VMEM((grouped, count * rows, depth), jnp.bfloat16)
    dma = pltpu.SemaphoreType.DMA
    out = pl.pallas_call(
        functools.partial(fused_kernel, count, blocks),
        out_shape=jax.ShapeDtypeStruct((rows, width), jnp.bfloat16),
        in_specs=[pl.BlockSpec(memory_space=pl.ANY)] * len(held),
        out_specs=pl.BlockSpec(memory_space=pl.ANY),
        scratch_shapes=[
            pltpu.SMEM(noise_level.shape, jnp.int32),
            pltpu.SMEM(decay_power.shape, jnp.int32),
            pltpu.VMEM(head_gain.shape, jnp.float32),
            dma((3,)),
            gathered,
            gathered,
            gathered,
            gathered,
            pltpu.VMEM((grouped, depth + 8, depth), jnp.float32),
            pltpu.VMEM((grouped, blocks - 1, depth + 8, depth), jnp.float32),
            dma((grouped, 3)),
            dma((grouped, 3)),
            dma((grouped,)),
            dma((1,)),
            dma((grouped,)),
            dma((grouped,)),
            dma((2,)),
            pltpu.SemaphoreType.REGULAR((count,)),
            pltpu.SemaphoreType.REGULAR,
            pltpu.SemaphoreType.REGULAR,
        ],
        compiler_params=pltpu.CompilerParams(collective_id=0, has_side_effects=True, vmem_limit_bytes=VMEM_GRANT),
        name="heads_exchange",
    )(*held)
    return out[None]


def body(queries, key_rows, value_rows, noise_level, decay_power, head_gain):
    heads_total = decay_power.shape[0]
    depth = head_gain.shape[1]
    local_rows = queries.shape[1]
    quarters = lax.axis_size("space") // HGROUPS
    grouped = heads_total // HGROUPS
    query_items = spread_items(queries[0], quarters, heads_total, depth)
    keys_sent = copied_items(key_rows[0], quarters, heads_total, depth)
    values_sent = copied_items(value_rows[0], quarters, heads_total, depth)
    query_got, keys_got, values_got = (
        lax.all_to_all(query_items, "space", split_axis=0, concat_axis=1, tiled=True),
        lax.all_to_all(keys_sent, "space", split_axis=0, concat_axis=1, tiled=True),
        lax.all_to_all(values_sent, "space", split_axis=0, concat_axis=1, tiled=True),
    )
    key_count = keys_got.shape[1]
    fresh = (
        jnp.einsum("inh,ine->ihe", keys_got, values_got, preferred_element_type=jnp.float32)
        / key_count
    )
    group_index = lax.axis_index("space") % HGROUPS
    powers = lax.dynamic_slice_in_dim(decay_power, group_index * grouped, grouped).astype(
        jnp.float32
    )
    level_now = noise_level[0].astype(jnp.float32)
    block_count = lax.axis_size("tm")
    rate = jnp.exp2(-(powers * (0.25 + 1.75 * level_now / LEVELS)) / block_count)
    zeros_state = jnp.zeros_like(fresh)
    unused_rate, before = carried_in(
        (rate, fresh), "tm", compose, (jnp.ones_like(rate), zeros_state)
    )
    state = (rate[:, None, None] * before).astype(jnp.bfloat16)
    gain_rows = lax.dynamic_slice_in_dim(head_gain, group_index * grouped, grouped)
    outcome = lax.map(attend_head, (query_got, keys_got, values_got, state, gain_rows))
    returned = lax.all_to_all(outcome, "space", split_axis=1, concat_axis=0, tiled=True)
    part_rows = local_rows // quarters
    restored = returned.reshape(quarters, heads_total, part_rows, depth).transpose(0, 2, 1, 3)
    return restored.reshape(1, local_rows, heads_total * depth)


def solution(mesh):
    in_specs = (
        P("tm", "space", None),
        P("tm", "space", None),
        P("tm", "space", None),
        P("tm"),
        P(),
        P(),
    )
    out_specs = P("tm", "space", None)
    step = fused if mesh.shape["space"] == HGROUPS else body
    return jax.shard_map(step, mesh=mesh, in_specs=in_specs, out_specs=out_specs, check_vma=False)
```

```python
import functools

import jax
import jax.numpy as jnp
from jax import lax
from jax.experimental import pallas as pl
from jax.experimental.pallas import tpu as pltpu
from jax.sharding import PartitionSpec as P

LEVELS = 1000
HGROUPS = 8
VMEM_GRANT = 32 * 2**20


epsilon = 1e-06


def carried_in(value, axis, join, neutral):
    count, mine = (lax.axis_size(axis), lax.axis_index(axis))
    pieces = jax.tree.map(lambda part: lax.all_gather(part, axis), value)
    so_far = jax.tree.map(
        lambda part, zero: jnp.full_like(part, 0) + jnp.asarray(zero, part.dtype), value, neutral
    )

    def lap(position, so_far):
        longer = join(so_far, jax.tree.map(lambda part: part[position], pieces))
        return jax.tree.map(lambda new, old: jnp.where(position < mine, new, old), longer, so_far)

    return lax.fori_loop(0, count - 1, lap, so_far)


def spread_items(block, quarters, heads_total, depth):
    part_rows = block.shape[0] // quarters
    shaped = block.reshape(quarters, part_rows, heads_total, depth).transpose(0, 2, 1, 3)
    return shaped.reshape(quarters * heads_total, part_rows, depth)


def copied_items(block, quarters, heads_total, depth):
    every = block.reshape(block.shape[0], heads_total, depth).transpose(1, 0, 2)
    copied = jnp.broadcast_to(every[None], (quarters,) + every.shape)
    return copied.reshape(quarters * heads_total, block.shape[0], depth)


def attend_head(bundle):
    query, key_item, value_item, state, gain_row = bundle
    factor = query.shape[1] ** (-0.5)
    scores = jnp.dot(query, key_item.T, preferred_element_type=jnp.float32) * factor
    row_top = jnp.max(scores, axis=1, keepdims=True)
    weights = jnp.exp(scores - row_top)
    row_total = jnp.sum(weights, axis=1, keepdims=True)
    numerator = jnp.dot(
        weights.astype(jnp.bfloat16), value_item, preferred_element_type=jnp.float32
    )
    carried = jnp.dot(query, state, preferred_element_type=jnp.float32) * factor
    mixed = numerator / row_total + carried
    normed = mixed * lax.rsqrt(jnp.mean(mixed * mixed, axis=1, keepdims=True) + epsilon) * gain_row
    return normed.astype(jnp.bfloat16)


def compose(earlier, later):
    return (earlier[0] * later[0], later[0][:, None, None] * earlier[1] + later[1])


MESH = pl.DeviceIdType.MESH


def fused_kernel(
    count, blocks, q_ref, k_ref, v_ref, noise_hbm, power_hbm, gain_hbm, out_ref,
    noise_ref, power_ref, gain_ref, small_done,
    q_all, k_all, v_all, outcome, fresh_mine, fresh_got,
    in_send, in_recv, out_send, out_recv, fresh_send, fresh_recv,
    first_keys, first_done, first_send, ready, column_ready, all_ready,
):
    rows = q_ref.shape[0]
    depth = gain_ref.shape[1]
    grouped = q_all.shape[0]
    total_rows = count * rows
    factor = depth ** (-0.5)
    me, now = lax.axis_index("space"), lax.axis_index("tm")
    chips, half = count // 2, count // 4
    chip, core = me // 2, me % 2

    def place(device):
        return device + 1 - 2 * (device % 2)

    rank = place(me)

    def at_space(device):
        return {"device_id": {"space": device}, "device_id_type": MESH}

    def at_tm(step):
        return {"device_id": {"tm": lax.rem(now + step, blocks)}, "device_id_type": MESH}

    low = chip < half
    targets = []
    for k in range(chips):
        if k == 0:
            below = chip
        elif k < half:
            below = k - 1 + jnp.where(k - 1 >= chip, 1, 0)
        else:
            below = k
        above = half - 1 - k if k < half else k
        there = jnp.where(low, below, above)
        targets.append((there, 2 * there + core, 2 * there + 1 - core))

    small = [
        pltpu.make_async_copy(held, here, small_done.at[index])
        for index, (held, here) in enumerate(
            ((noise_hbm, noise_ref), (power_hbm, power_ref), (gain_hbm, gain_ref))
        )
    ]

    barrier = pltpu.get_barrier_semaphore()
    is_hub = rank == 0
    is_last = chip == chips - 1
    for other in range(count - 1, -1, -1):

        @pl.when(jnp.logical_and(me != other, jnp.logical_or(jnp.logical_not(is_last), place(other) > rank)))
        def _():
            pl.semaphore_signal(barrier, inc=1, **at_space(other))

    @pl.when(is_hub)
    def _():
        for step in range(1, blocks):
            pl.semaphore_signal(barrier, inc=1, **at_tm(step))

    @pl.when(low)
    def _():
        for device in range(count):
            pltpu.make_async_copy(
                k_ref.at[:, pl.ds(device * grouped * depth, depth)], first_keys.at[device], first_done
            ).start()

    pl.semaphore_wait(
        barrier, jnp.where(is_last, rank, count - 3 + jnp.where(is_hub, blocks - 1, 0))
    )

    @pl.when(is_last)
    def _():
        for other in range(count):

            @pl.when(place(other) < rank)
            def _():
                pl.semaphore_signal(ready.at[me], inc=1, **at_space(other))

    def lanes(head):
        return pl.ds(pl.multiple_of(head * depth, depth), depth)

    def part(device):
        return pl.ds(pl.multiple_of(device * rows, rows), rows)

    arrays = ((k_ref, k_all), (v_ref, v_all), (q_ref, q_all))

    @pl.when(low)
    def _():
        pltpu.make_async_copy(first_keys, first_keys, first_done).wait()

    def send_input(device, slot, which):
        source, target = arrays[which]

        def send(piece):
            pltpu.make_async_remote_copy(
                src_ref=piece,
                dst_ref=target.at[slot, part(me)],
                send_sem=in_send.at[slot, which],
                recv_sem=in_recv.at[slot, which],
                **at_space(device),
            ).start()

        piece = source.at[:, lanes(device * grouped + slot)]
        if slot == 0 and which == 0:

            @pl.when(low)
            def _():
                send(first_keys.at[device])

            @pl.when(jnp.logical_not(low))
            def _():
                send(piece)
        else:
            send(piece)

    def send_chip(position, slot, which):
        there, same, opposite = targets[position]

        @pl.when(there != chip)
        def _():
            send_input(same, slot, which)

        send_input(opposite, slot, which)

    for slot in range(grouped):
        known = chips - 1 if slot == 0 else chips
        for which in range(len(arrays)):
            for position in range(known):
                send_chip(position, slot, which)
        if slot == 0:
            for device in (count - 2, count - 1):

                @pl.when(place(device) > rank)
                def _():
                    pl.semaphore_wait(ready.at[device], 1)

            for which in range(len(arrays)):
                send_chip(chips - 1, slot, which)

    for slot in range(grouped):
        for which, (source, target) in enumerate(arrays):
            pltpu.make_async_copy(
                source.at[:, lanes(me * grouped + slot)],
                target.at[slot, part(me)],
                in_recv.at[slot, which],
            ).start()

    for copy in small:
        copy.start()

    @pl.when(is_hub)
    def _():
        for step in range(1, blocks):
            pl.semaphore_signal(column_ready, inc=1, **at_tm(step))
        pl.semaphore_wait(column_ready, blocks - 1)
        for other in range(count):
            if place(other) > 0:
                pl.semaphore_signal(all_ready, inc=1, **at_space(other))

    @pl.when(rank > 0)
    def _():
        pl.semaphore_wait(all_ready, 1)

    def arrived(slot, which):
        whole = arrays[which][1].at[slot]
        pltpu.make_async_copy(whole, whole, in_recv.at[slot, which]).wait()

    def give_back(slot, device, done=None):
        pltpu.make_async_remote_copy(
            src_ref=outcome.at[slot, part(device)],
            dst_ref=out_ref.at[:, lanes(me * grouped + slot)],
            send_sem=out_send.at[slot] if done is None else done,
            recv_sem=out_recv.at[0],
            **at_space(device),
        ).start()

    far_chips = [jnp.where(low, half + k, k) for k in range(half)]
    near_chips = [half * jnp.where(low, 0, 1) + k for k in range(half)]

    def give_far(slot, which):
        for digit in range(2):
            give_back(
                slot, 2 * far_chips[which] + digit,
                first_send.at[slot // (grouped - 1)] if which == 0 else None,
            )

    at_end = jnp.logical_or(chip == 0, chip == chips - 1)

    def give_earlier():
        for earlier in range(grouped - 1):
            give_far(earlier, 0)
        for earlier in range(grouped - 2):
            give_far(earlier, 1)
        give_back(grouped - 2, 2 * far_chips[1])

        @pl.when(core == 0)
        def _():
            give_back(grouped - 2, 2 * far_chips[1] + 1)

    def give_near(slot):
        for there in near_chips:

            @pl.when(there != chip)
            def _():
                give_back(slot, 2 * there)
                give_back(slot, 2 * there + 1)

        give_back(slot, 2 * chip + 1 - core)

    for copy in small:
        copy.wait()
    level = jnp.full((8, depth), noise_ref[0], jnp.int32).astype(jnp.float32)
    for slot in range(grouped):
        head = me * grouped + slot
        power = jnp.full((8, depth), power_ref[head], jnp.int32).astype(jnp.float32)
        rate = jnp.exp2(-(power * (0.25 + 1.75 * level / LEVELS)) / blocks)
        arrived(slot, 0)
        arrived(slot, 1)
        fresh = lax.dot_general(
            k_all[slot], v_all[slot], (((0,), (0,)), ((), ())), preferred_element_type=jnp.float32
        )
        fresh_mine[slot, 0:depth, :] = fresh / total_rows
        fresh_mine[slot, depth : depth + 8, :] = rate
        for step in range(1, blocks):
            pltpu.make_async_remote_copy(
                src_ref=fresh_mine.at[slot],
                dst_ref=fresh_got.at[slot, step - 1],
                send_sem=fresh_send.at[slot],
                recv_sem=fresh_recv.at[slot],
                **at_tm(step),
            ).start()
        arrived(slot, 2)
        if slot == grouped - 1:
            @pl.when(at_end)
            def _():
                give_earlier()

        landed = fresh_got.at[slot]
        pltpu.make_async_copy(landed, landed, fresh_recv.at[slot]).wait()
        carried = jnp.zeros((depth, depth), jnp.float32)
        for step in range(blocks - 1, 0, -1):
            longer = (
                fresh_got[slot, step - 1, depth : depth + 1, :] * carried
                + fresh_got[slot, step - 1, 0:depth, :]
            )
            carried = jnp.where(now - step >= 0, longer, carried)
        state = (rate[0:1, :] * carried).astype(jnp.bfloat16)
        gain_row = gain_ref[pl.ds(head, 1), :]

        def attend(first_chip):
            span = pl.ds(pl.multiple_of(first_chip * 2 * rows, 2 * half * rows), 2 * half * rows)
            query = q_all[slot, span, :]
            scores = lax.dot_general(
                query, k_all[slot], (((1,), (1,)), ((), ())), preferred_element_type=jnp.float32
            ) * factor
            weights = jnp.exp(scores - jnp.max(scores, axis=1, keepdims=True))
            row_total = jnp.sum(weights, axis=1, keepdims=True)
            numerator = jnp.dot(
                weights.astype(jnp.bfloat16), v_all[slot], preferred_element_type=jnp.float32
            )
            before = jnp.dot(query, state, preferred_element_type=jnp.float32) * factor
            mixed = numerator / row_total + before
            scale = lax.rsqrt(jnp.mean(mixed * mixed, axis=1, keepdims=True) + epsilon)
            outcome[slot, span, :] = (mixed * scale * gain_row).astype(jnp.bfloat16)

        attend(half * jnp.where(low, 1, 0))
        if slot == grouped - 1:
            give_far(slot, 0)
        attend(near_chips[0])
        give_near(slot)
        if slot == grouped - 2:
            @pl.when(jnp.logical_not(at_end))
            def _():
                give_earlier()

        if slot == grouped - 1:
            @pl.when(jnp.logical_not(low))
            def _():
                first = outcome.at[0, pl.ds(0, 2 * rows * (grouped - 1))]
                pltpu.make_async_copy(first, first, first_send.at[0]).wait()

            @pl.when(jnp.logical_not(core == 0))
            def _():
                give_back(grouped - 2, 2 * far_chips[1] + 1)

            give_far(slot, 1)
        pltpu.make_async_copy(
            outcome.at[slot, part(me)], out_ref.at[:, lanes(head)], out_recv.at[0]
        ).start()

    @pl.when(low)
    def _():
        first = outcome.at[0, pl.ds(0, 2 * rows * (grouped - 1))]
        pltpu.make_async_copy(first, first, first_send.at[0]).wait()

    last = outcome.at[0, pl.ds(0, 2 * rows)]
    pltpu.make_async_copy(last, last, first_send.at[1]).wait()
    for slot in range(grouped):
        for which in range(len(arrays)):
            sent = arrays[which][1].at[slot, pl.ds(0, total_rows - rows)]
            pltpu.make_async_copy(sent, sent, in_send.at[slot, which]).wait()
        landed = fresh_got.at[slot]
        pltpu.make_async_copy(landed, landed, fresh_send.at[slot]).wait()
        returned = outcome.at[slot, pl.ds(0, total_rows - 3 * rows)]
        pltpu.make_async_copy(returned, returned, out_send.at[slot]).wait()
    pltpu.make_async_copy(out_ref, out_ref, out_recv.at[0]).wait()


def fused(queries, key_rows, value_rows, noise_level, decay_power, head_gain):
    count, blocks = lax.axis_size("space"), lax.axis_size("tm")
    rows, width = queries.shape[1:]
    heads_total, depth = head_gain.shape
    grouped = heads_total // count
    held = [
        pltpu.with_memory_space_constraint(operand, pltpu.HBM)
        for operand in (queries[0], key_rows[0], value_rows[0], decay_power, head_gain)
    ]
    held.insert(3, noise_level)
    gathered = pltpu.VMEM((grouped, count * rows, depth), jnp.bfloat16)
    dma = pltpu.SemaphoreType.DMA
    out = pl.pallas_call(
        functools.partial(fused_kernel, count, blocks),
        out_shape=jax.ShapeDtypeStruct((rows, width), jnp.bfloat16),
        in_specs=[pl.BlockSpec(memory_space=pl.ANY)] * len(held),
        out_specs=pl.BlockSpec(memory_space=pl.ANY),
        scratch_shapes=[
            pltpu.SMEM(noise_level.shape, jnp.int32),
            pltpu.SMEM(decay_power.shape, jnp.int32),
            pltpu.VMEM(head_gain.shape, jnp.float32),
            dma((3,)),
            gathered,
            gathered,
            gathered,
            gathered,
            pltpu.VMEM((grouped, depth + 8, depth), jnp.float32),
            pltpu.VMEM((grouped, blocks - 1, depth + 8, depth), jnp.float32),
            dma((grouped, 3)),
            dma((grouped, 3)),
            dma((grouped,)),
            dma((1,)),
            dma((grouped,)),
            dma((grouped,)),
            pltpu.VMEM((count, rows, depth), jnp.bfloat16),
            pltpu.SemaphoreType.DMA,
            dma((2,)),
            pltpu.SemaphoreType.REGULAR((count,)),
            pltpu.SemaphoreType.REGULAR,
            pltpu.SemaphoreType.REGULAR,
        ],
        compiler_params=pltpu.CompilerParams(collective_id=0, has_side_effects=True, vmem_limit_bytes=VMEM_GRANT),
        name="heads_exchange",
    )(*held)
    return out[None]


def body(queries, key_rows, value_rows, noise_level, decay_power, head_gain):
    heads_total = decay_power.shape[0]
    depth = head_gain.shape[1]
    local_rows = queries.shape[1]
    quarters = lax.axis_size("space") // HGROUPS
    grouped = heads_total // HGROUPS
    query_items = spread_items(queries[0], quarters, heads_total, depth)
    keys_sent = copied_items(key_rows[0], quarters, heads_total, depth)
    values_sent = copied_items(value_rows[0], quarters, heads_total, depth)
    query_got, keys_got, values_got = (
        lax.all_to_all(query_items, "space", split_axis=0, concat_axis=1, tiled=True),
        lax.all_to_all(keys_sent, "space", split_axis=0, concat_axis=1, tiled=True),
        lax.all_to_all(values_sent, "space", split_axis=0, concat_axis=1, tiled=True),
    )
    key_count = keys_got.shape[1]
    fresh = (
        jnp.einsum("inh,ine->ihe", keys_got, values_got, preferred_element_type=jnp.float32)
        / key_count
    )
    group_index = lax.axis_index("space") % HGROUPS
    powers = lax.dynamic_slice_in_dim(decay_power, group_index * grouped, grouped).astype(
        jnp.float32
    )
    level_now = noise_level[0].astype(jnp.float32)
    block_count = lax.axis_size("tm")
    rate = jnp.exp2(-(powers * (0.25 + 1.75 * level_now / LEVELS)) / block_count)
    zeros_state = jnp.zeros_like(fresh)
    unused_rate, before = carried_in(
        (rate, fresh), "tm", compose, (jnp.ones_like(rate), zeros_state)
    )
    state = (rate[:, None, None] * before).astype(jnp.bfloat16)
    gain_rows = lax.dynamic_slice_in_dim(head_gain, group_index * grouped, grouped)
    outcome = lax.map(attend_head, (query_got, keys_got, values_got, state, gain_rows))
    returned = lax.all_to_all(outcome, "space", split_axis=1, concat_axis=0, tiled=True)
    part_rows = local_rows // quarters
    restored = returned.reshape(quarters, heads_total, part_rows, depth).transpose(0, 2, 1, 3)
    return restored.reshape(1, local_rows, heads_total * depth)


def solution(mesh):
    in_specs = (
        P("tm", "space", None),
        P("tm", "space", None),
        P("tm", "space", None),
        P("tm"),
        P(),
        P(),
    )
    out_specs = P("tm", "space", None)
    step = fused if mesh.shape["space"] == HGROUPS else body
    return jax.shard_map(step, mesh=mesh, in_specs=in_specs, out_specs=out_specs, check_vma=False)
```

```python
import functools

import jax
import jax.numpy as jnp
from jax import lax
from jax.experimental import pallas as pl
from jax.experimental.pallas import tpu as pltpu
from jax.sharding import PartitionSpec as P

LEVELS = 1000
HGROUPS = 8
VMEM_GRANT = 32 * 2**20


epsilon = 1e-06


def carried_in(value, axis, join, neutral):
    count, mine = (lax.axis_size(axis), lax.axis_index(axis))
    pieces = jax.tree.map(lambda part: lax.all_gather(part, axis), value)
    so_far = jax.tree.map(
        lambda part, zero: jnp.full_like(part, 0) + jnp.asarray(zero, part.dtype), value, neutral
    )

    def lap(position, so_far):
        longer = join(so_far, jax.tree.map(lambda part: part[position], pieces))
        return jax.tree.map(lambda new, old: jnp.where(position < mine, new, old), longer, so_far)

    return lax.fori_loop(0, count - 1, lap, so_far)


def spread_items(block, quarters, heads_total, depth):
    part_rows = block.shape[0] // quarters
    shaped = block.reshape(quarters, part_rows, heads_total, depth).transpose(0, 2, 1, 3)
    return shaped.reshape(quarters * heads_total, part_rows, depth)


def copied_items(block, quarters, heads_total, depth):
    every = block.reshape(block.shape[0], heads_total, depth).transpose(1, 0, 2)
    copied = jnp.broadcast_to(every[None], (quarters,) + every.shape)
    return copied.reshape(quarters * heads_total, block.shape[0], depth)


def attend_head(bundle):
    query, key_item, value_item, state, gain_row = bundle
    factor = query.shape[1] ** (-0.5)
    scores = jnp.dot(query, key_item.T, preferred_element_type=jnp.float32) * factor
    row_top = jnp.max(scores, axis=1, keepdims=True)
    weights = jnp.exp(scores - row_top)
    row_total = jnp.sum(weights, axis=1, keepdims=True)
    numerator = jnp.dot(
        weights.astype(jnp.bfloat16), value_item, preferred_element_type=jnp.float32
    )
    carried = jnp.dot(query, state, preferred_element_type=jnp.float32) * factor
    mixed = numerator / row_total + carried
    normed = mixed * lax.rsqrt(jnp.mean(mixed * mixed, axis=1, keepdims=True) + epsilon) * gain_row
    return normed.astype(jnp.bfloat16)


def compose(earlier, later):
    return (earlier[0] * later[0], later[0][:, None, None] * earlier[1] + later[1])


MESH = pl.DeviceIdType.MESH


def fused_kernel(
    count, blocks, q_ref, k_ref, v_ref, noise_hbm, power_hbm, gain_hbm, out_ref,
    noise_ref, power_ref, gain_ref, small_done,
    q_all, k_all, v_all, outcome, fresh_mine, fresh_got,
    in_send, in_recv, out_send, out_recv, fresh_send, fresh_recv,
    first_keys, first_done, first_send, ready, column_ready, all_ready,
):
    rows = q_ref.shape[0]
    depth = gain_ref.shape[1]
    grouped = q_all.shape[0]
    total_rows = count * rows
    factor = depth ** (-0.5)
    me, now = lax.axis_index("space"), lax.axis_index("tm")
    chips, half = count // 2, count // 4
    chip, core = me // 2, me % 2

    def place(device):
        return device + 1 - 2 * (device % 2)

    rank = place(me)

    def at_space(device):
        return {"device_id": {"space": device}, "device_id_type": MESH}

    def at_tm(step):
        return {"device_id": {"tm": lax.rem(now + step, blocks)}, "device_id_type": MESH}

    low = chip < half
    targets = []
    for k in range(chips):
        if k == 0:
            below = chip
        elif k < half:
            below = k - 1 + jnp.where(k - 1 >= chip, 1, 0)
        else:
            below = k
        above = half - 1 - k if k < half else k
        there = jnp.where(low, below, above)
        targets.append((there, 2 * there + core, 2 * there + 1 - core))

    small = [
        pltpu.make_async_copy(held, here, small_done.at[index])
        for index, (held, here) in enumerate(
            ((noise_hbm, noise_ref), (power_hbm, power_ref), (gain_hbm, gain_ref))
        )
    ]

    barrier = pltpu.get_barrier_semaphore()
    is_hub = rank == 0
    is_last = chip == chips - 1
    for other in range(count - 1, -1, -1):

        @pl.when(jnp.logical_and(me != other, jnp.logical_or(jnp.logical_not(is_last), place(other) > rank)))
        def _():
            pl.semaphore_signal(barrier, inc=1, **at_space(other))

    @pl.when(is_hub)
    def _():
        for step in range(1, blocks):
            pl.semaphore_signal(barrier, inc=1, **at_tm(step))

    @pl.when(low)
    def _():
        for device in range(count):
            pltpu.make_async_copy(
                k_ref.at[:, pl.ds(device * grouped * depth, depth)], first_keys.at[device], first_done
            ).start()

    pl.semaphore_wait(
        barrier, jnp.where(is_last, rank, count - 3 + jnp.where(is_hub, blocks - 1, 0))
    )

    @pl.when(is_last)
    def _():
        for other in range(count):

            @pl.when(place(other) < rank)
            def _():
                pl.semaphore_signal(ready.at[me], inc=1, **at_space(other))

    def lanes(head):
        return pl.ds(pl.multiple_of(head * depth, depth), depth)

    def part(device):
        return pl.ds(pl.multiple_of(device * rows, rows), rows)

    arrays = ((k_ref, k_all), (v_ref, v_all), (q_ref, q_all))

    @pl.when(low)
    def _():
        pltpu.make_async_copy(first_keys, first_keys, first_done).wait()

    def send_input(device, slot, which):
        source, target = arrays[which]

        def send(piece):
            pltpu.make_async_remote_copy(
                src_ref=piece,
                dst_ref=target.at[slot, part(me)],
                send_sem=in_send.at[slot, which],
                recv_sem=in_recv.at[slot, which],
                **at_space(device),
            ).start()

        piece = source.at[:, lanes(device * grouped + slot)]
        if slot == 0 and which == 0:

            @pl.when(low)
            def _():
                send(first_keys.at[device])

            @pl.when(jnp.logical_not(low))
            def _():
                send(piece)
        else:
            send(piece)

    def send_chip(position, slot, which):
        there, same, opposite = targets[position]

        @pl.when(there != chip)
        def _():
            send_input(same, slot, which)

        send_input(opposite, slot, which)

    for slot in range(grouped):
        known = chips - 1 if slot == 0 else chips
        for which in range(len(arrays)):
            for position in range(known):
                send_chip(position, slot, which)
        if slot == 0:
            for device in (count - 2, count - 1):

                @pl.when(place(device) > rank)
                def _():
                    pl.semaphore_wait(ready.at[device], 1)

            for which in range(len(arrays)):
                send_chip(chips - 1, slot, which)

    for slot in range(grouped):
        for which, (source, target) in enumerate(arrays):
            pltpu.make_async_copy(
                source.at[:, lanes(me * grouped + slot)],
                target.at[slot, part(me)],
                in_recv.at[slot, which],
            ).start()

    for copy in small:
        copy.start()

    @pl.when(is_hub)
    def _():
        for step in range(1, blocks):
            pl.semaphore_signal(column_ready, inc=1, **at_tm(step))
        pl.semaphore_wait(column_ready, blocks - 1)
        for other in range(count):
            if place(other) > 0:
                pl.semaphore_signal(all_ready, inc=1, **at_space(other))

    @pl.when(rank > 0)
    def _():
        pl.semaphore_wait(all_ready, 1)

    def arrived(slot, which):
        whole = arrays[which][1].at[slot]
        pltpu.make_async_copy(whole, whole, in_recv.at[slot, which]).wait()

    def give_back(slot, device, done=None):
        pltpu.make_async_remote_copy(
            src_ref=outcome.at[slot, part(device)],
            dst_ref=out_ref.at[:, lanes(me * grouped + slot)],
            send_sem=out_send.at[slot] if done is None else done,
            recv_sem=out_recv.at[0],
            **at_space(device),
        ).start()

    far_chips = [jnp.where(low, half + k, k) for k in range(half)]
    near_chips = [half * jnp.where(low, 0, 1) + k for k in range(half)]

    def give_far(slot, which):
        for digit in range(2):
            give_back(
                slot, 2 * far_chips[which] + digit,
                first_send.at[slot // (grouped - 1)] if which == 0 else None,
            )

    at_end = jnp.logical_or(chip == 0, chip == chips - 1)

    def give_first():
        for earlier in range(grouped - 2):
            give_far(earlier, 0)
            give_far(earlier, 1)

    def give_earlier():
        give_far(grouped - 2, 0)
        give_back(grouped - 2, 2 * far_chips[1])

        @pl.when(core == 0)
        def _():
            give_back(grouped - 2, 2 * far_chips[1] + 1)

    def give_near(slot):
        for there in near_chips:

            @pl.when(there != chip)
            def _():
                give_back(slot, 2 * there)
                give_back(slot, 2 * there + 1)

        give_back(slot, 2 * chip + 1 - core)

    for copy in small:
        copy.wait()
    level = jnp.full((8, depth), noise_ref[0], jnp.int32).astype(jnp.float32)
    for slot in range(grouped):
        head = me * grouped + slot
        power = jnp.full((8, depth), power_ref[head], jnp.int32).astype(jnp.float32)
        rate = jnp.exp2(-(power * (0.25 + 1.75 * level / LEVELS)) / blocks)
        arrived(slot, 0)
        arrived(slot, 1)
        fresh = lax.dot_general(
            k_all[slot], v_all[slot], (((0,), (0,)), ((), ())), preferred_element_type=jnp.float32
        )
        fresh_mine[slot, 0:depth, :] = fresh / total_rows
        fresh_mine[slot, depth : depth + 8, :] = rate
        for step in range(1, blocks):
            pltpu.make_async_remote_copy(
                src_ref=fresh_mine.at[slot],
                dst_ref=fresh_got.at[slot, step - 1],
                send_sem=fresh_send.at[slot],
                recv_sem=fresh_recv.at[slot],
                **at_tm(step),
            ).start()
        arrived(slot, 2)
        if slot == grouped - 1:
            @pl.when(at_end)
            def _():
                give_first()
                give_earlier()

        landed = fresh_got.at[slot]
        pltpu.make_async_copy(landed, landed, fresh_recv.at[slot]).wait()
        carried = jnp.zeros((depth, depth), jnp.float32)
        for step in range(blocks - 1, 0, -1):
            longer = (
                fresh_got[slot, step - 1, depth : depth + 1, :] * carried
                + fresh_got[slot, step - 1, 0:depth, :]
            )
            carried = jnp.where(now - step >= 0, longer, carried)
        state = (rate[0:1, :] * carried).astype(jnp.bfloat16)
        gain_row = gain_ref[pl.ds(head, 1), :]

        def attend(first_chip):
            span = pl.ds(pl.multiple_of(first_chip * 2 * rows, 2 * half * rows), 2 * half * rows)
            query = q_all[slot, span, :]
            scores = lax.dot_general(
                query, k_all[slot], (((1,), (1,)), ((), ())), preferred_element_type=jnp.float32
            ) * factor
            weights = jnp.exp(scores - jnp.max(scores, axis=1, keepdims=True))
            row_total = jnp.sum(weights, axis=1, keepdims=True)
            numerator = jnp.dot(
                weights.astype(jnp.bfloat16), v_all[slot], preferred_element_type=jnp.float32
            )
            before = jnp.dot(query, state, preferred_element_type=jnp.float32) * factor
            mixed = numerator / row_total + before
            scale = lax.rsqrt(jnp.mean(mixed * mixed, axis=1, keepdims=True) + epsilon)
            outcome[slot, span, :] = (mixed * scale * gain_row).astype(jnp.bfloat16)

        attend(half * jnp.where(low, 1, 0))
        if slot == grouped - 1:
            give_far(slot, 0)
        attend(near_chips[0])
        give_near(slot)
        if slot == grouped - 3:
            @pl.when(jnp.logical_not(at_end))
            def _():
                give_first()

        if slot == grouped - 2:
            @pl.when(jnp.logical_not(at_end))
            def _():
                give_earlier()

        if slot == grouped - 1:
            @pl.when(jnp.logical_not(low))
            def _():
                first = outcome.at[0, pl.ds(0, 2 * rows * (grouped - 1))]
                pltpu.make_async_copy(first, first, first_send.at[0]).wait()

            @pl.when(jnp.logical_not(core == 0))
            def _():
                give_back(grouped - 2, 2 * far_chips[1] + 1)

            give_far(slot, 1)
        pltpu.make_async_copy(
            outcome.at[slot, part(me)], out_ref.at[:, lanes(head)], out_recv.at[0]
        ).start()

    @pl.when(low)
    def _():
        first = outcome.at[0, pl.ds(0, 2 * rows * (grouped - 1))]
        pltpu.make_async_copy(first, first, first_send.at[0]).wait()

    last = outcome.at[0, pl.ds(0, 2 * rows)]
    pltpu.make_async_copy(last, last, first_send.at[1]).wait()
    for slot in range(grouped):
        for which in range(len(arrays)):
            sent = arrays[which][1].at[slot, pl.ds(0, total_rows - rows)]
            pltpu.make_async_copy(sent, sent, in_send.at[slot, which]).wait()
        landed = fresh_got.at[slot]
        pltpu.make_async_copy(landed, landed, fresh_send.at[slot]).wait()
        returned = outcome.at[slot, pl.ds(0, total_rows - 3 * rows)]
        pltpu.make_async_copy(returned, returned, out_send.at[slot]).wait()
    pltpu.make_async_copy(out_ref, out_ref, out_recv.at[0]).wait()


def fused(queries, key_rows, value_rows, noise_level, decay_power, head_gain):
    count, blocks = lax.axis_size("space"), lax.axis_size("tm")
    rows, width = queries.shape[1:]
    heads_total, depth = head_gain.shape
    grouped = heads_total // count
    held = [
        pltpu.with_memory_space_constraint(operand, pltpu.HBM)
        for operand in (queries[0], key_rows[0], value_rows[0], decay_power, head_gain)
    ]
    held.insert(3, noise_level)
    gathered = pltpu.VMEM((grouped, count * rows, depth), jnp.bfloat16)
    dma = pltpu.SemaphoreType.DMA
    out = pl.pallas_call(
        functools.partial(fused_kernel, count, blocks),
        out_shape=jax.ShapeDtypeStruct((rows, width), jnp.bfloat16),
        in_specs=[pl.BlockSpec(memory_space=pl.ANY)] * len(held),
        out_specs=pl.BlockSpec(memory_space=pl.ANY),
        scratch_shapes=[
            pltpu.SMEM(noise_level.shape, jnp.int32),
            pltpu.SMEM(decay_power.shape, jnp.int32),
            pltpu.VMEM(head_gain.shape, jnp.float32),
            dma((3,)),
            gathered,
            gathered,
            gathered,
            gathered,
            pltpu.VMEM((grouped, depth + 8, depth), jnp.float32),
            pltpu.VMEM((grouped, blocks - 1, depth + 8, depth), jnp.float32),
            dma((grouped, 3)),
            dma((grouped, 3)),
            dma((grouped,)),
            dma((1,)),
            dma((grouped,)),
            dma((grouped,)),
            pltpu.VMEM((count, rows, depth), jnp.bfloat16),
            pltpu.SemaphoreType.DMA,
            dma((2,)),
            pltpu.SemaphoreType.REGULAR((count,)),
            pltpu.SemaphoreType.REGULAR,
            pltpu.SemaphoreType.REGULAR,
        ],
        compiler_params=pltpu.CompilerParams(collective_id=0, has_side_effects=True, vmem_limit_bytes=VMEM_GRANT),
        name="heads_exchange",
    )(*held)
    return out[None]


def body(queries, key_rows, value_rows, noise_level, decay_power, head_gain):
    heads_total = decay_power.shape[0]
    depth = head_gain.shape[1]
    local_rows = queries.shape[1]
    quarters = lax.axis_size("space") // HGROUPS
    grouped = heads_total // HGROUPS
    query_items = spread_items(queries[0], quarters, heads_total, depth)
    keys_sent = copied_items(key_rows[0], quarters, heads_total, depth)
    values_sent = copied_items(value_rows[0], quarters, heads_total, depth)
    query_got, keys_got, values_got = (
        lax.all_to_all(query_items, "space", split_axis=0, concat_axis=1, tiled=True),
        lax.all_to_all(keys_sent, "space", split_axis=0, concat_axis=1, tiled=True),
        lax.all_to_all(values_sent, "space", split_axis=0, concat_axis=1, tiled=True),
    )
    key_count = keys_got.shape[1]
    fresh = (
        jnp.einsum("inh,ine->ihe", keys_got, values_got, preferred_element_type=jnp.float32)
        / key_count
    )
    group_index = lax.axis_index("space") % HGROUPS
    powers = lax.dynamic_slice_in_dim(decay_power, group_index * grouped, grouped).astype(
        jnp.float32
    )
    level_now = noise_level[0].astype(jnp.float32)
    block_count = lax.axis_size("tm")
    rate = jnp.exp2(-(powers * (0.25 + 1.75 * level_now / LEVELS)) / block_count)
    zeros_state = jnp.zeros_like(fresh)
    unused_rate, before = carried_in(
        (rate, fresh), "tm", compose, (jnp.ones_like(rate), zeros_state)
    )
    state = (rate[:, None, None] * before).astype(jnp.bfloat16)
    gain_rows = lax.dynamic_slice_in_dim(head_gain, group_index * grouped, grouped)
    outcome = lax.map(attend_head, (query_got, keys_got, values_got, state, gain_rows))
    returned = lax.all_to_all(outcome, "space", split_axis=1, concat_axis=0, tiled=True)
    part_rows = local_rows // quarters
    restored = returned.reshape(quarters, heads_total, part_rows, depth).transpose(0, 2, 1, 3)
    return restored.reshape(1, local_rows, heads_total * depth)


def solution(mesh):
    in_specs = (
        P("tm", "space", None),
        P("tm", "space", None),
        P("tm", "space", None),
        P("tm"),
        P(),
        P(),
    )
    out_specs = P("tm", "space", None)
    step = fused if mesh.shape["space"] == HGROUPS else body
    return jax.shard_map(step, mesh=mesh, in_specs=in_specs, out_specs=out_specs, check_vma=False)
```

```python
import functools

import jax
import jax.numpy as jnp
from jax import lax
from jax.experimental import pallas as pl
from jax.experimental.pallas import tpu as pltpu
from jax.sharding import PartitionSpec as P

LEVELS = 1000
HGROUPS = 8
VMEM_GRANT = 32 * 2**20


epsilon = 1e-06


def carried_in(value, axis, join, neutral):
    count, mine = (lax.axis_size(axis), lax.axis_index(axis))
    pieces = jax.tree.map(lambda part: lax.all_gather(part, axis), value)
    so_far = jax.tree.map(
        lambda part, zero: jnp.full_like(part, 0) + jnp.asarray(zero, part.dtype), value, neutral
    )

    def lap(position, so_far):
        longer = join(so_far, jax.tree.map(lambda part: part[position], pieces))
        return jax.tree.map(lambda new, old: jnp.where(position < mine, new, old), longer, so_far)

    return lax.fori_loop(0, count - 1, lap, so_far)


def spread_items(block, quarters, heads_total, depth):
    part_rows = block.shape[0] // quarters
    shaped = block.reshape(quarters, part_rows, heads_total, depth).transpose(0, 2, 1, 3)
    return shaped.reshape(quarters * heads_total, part_rows, depth)


def copied_items(block, quarters, heads_total, depth):
    every = block.reshape(block.shape[0], heads_total, depth).transpose(1, 0, 2)
    copied = jnp.broadcast_to(every[None], (quarters,) + every.shape)
    return copied.reshape(quarters * heads_total, block.shape[0], depth)


def attend_head(bundle):
    query, key_item, value_item, state, gain_row = bundle
    factor = query.shape[1] ** (-0.5)
    scores = jnp.dot(query, key_item.T, preferred_element_type=jnp.float32) * factor
    row_top = jnp.max(scores, axis=1, keepdims=True)
    weights = jnp.exp(scores - row_top)
    row_total = jnp.sum(weights, axis=1, keepdims=True)
    numerator = jnp.dot(
        weights.astype(jnp.bfloat16), value_item, preferred_element_type=jnp.float32
    )
    carried = jnp.dot(query, state, preferred_element_type=jnp.float32) * factor
    mixed = numerator / row_total + carried
    normed = mixed * lax.rsqrt(jnp.mean(mixed * mixed, axis=1, keepdims=True) + epsilon) * gain_row
    return normed.astype(jnp.bfloat16)


def compose(earlier, later):
    return (earlier[0] * later[0], later[0][:, None, None] * earlier[1] + later[1])


MESH = pl.DeviceIdType.MESH


def fused_kernel(
    count, blocks, q_ref, k_ref, v_ref, noise_hbm, power_hbm, gain_hbm, out_ref,
    noise_ref, power_ref, gain_ref, small_done,
    q_all, k_all, v_all, outcome, fresh_mine, fresh_got,
    in_send, in_recv, out_send, out_recv, fresh_send, fresh_recv,
    first_keys, first_done, first_send, ready, column_ready, all_ready,
):
    rows = q_ref.shape[0]
    depth = gain_ref.shape[1]
    grouped = q_all.shape[0]
    total_rows = count * rows
    factor = depth ** (-0.5)
    me, now = lax.axis_index("space"), lax.axis_index("tm")
    chips, half = count // 2, count // 4
    chip, core = me // 2, me % 2

    def place(device):
        return device + 1 - 2 * (device % 2)

    rank = place(me)

    def at_space(device):
        return {"device_id": {"space": device}, "device_id_type": MESH}

    def at_tm(step):
        return {"device_id": {"tm": lax.rem(now + step, blocks)}, "device_id_type": MESH}

    low = chip < half
    targets = []
    for k in range(chips):
        if k == 0:
            below = chip
        elif k < half:
            below = k - 1 + jnp.where(k - 1 >= chip, 1, 0)
        else:
            below = k
        above = half - 1 - k if k < half else k
        there = jnp.where(low, below, above)
        targets.append((there, 2 * there + core, 2 * there + 1 - core))

    small = [
        pltpu.make_async_copy(held, here, small_done.at[index])
        for index, (held, here) in enumerate(
            ((noise_hbm, noise_ref), (power_hbm, power_ref), (gain_hbm, gain_ref))
        )
    ]

    barrier = pltpu.get_barrier_semaphore()
    is_hub = rank == 0
    is_last = chip == chips - 1
    for other in range(count - 1, -1, -1):

        @pl.when(jnp.logical_and(me != other, jnp.logical_or(jnp.logical_not(is_last), place(other) > rank)))
        def _():
            pl.semaphore_signal(barrier, inc=1, **at_space(other))

    @pl.when(is_hub)
    def _():
        for step in range(1, blocks):
            pl.semaphore_signal(barrier, inc=1, **at_tm(step))

    @pl.when(low)
    def _():
        for device in range(count):
            pltpu.make_async_copy(
                k_ref.at[:, pl.ds(device * grouped * depth, depth)], first_keys.at[device], first_done
            ).start()

    pl.semaphore_wait(
        barrier, jnp.where(is_last, rank, count - 3 + jnp.where(is_hub, blocks - 1, 0))
    )

    @pl.when(is_last)
    def _():
        for other in range(count):

            @pl.when(place(other) < rank)
            def _():
                pl.semaphore_signal(ready.at[me], inc=1, **at_space(other))

    def lanes(head):
        return pl.ds(pl.multiple_of(head * depth, depth), depth)

    def part(device):
        return pl.ds(pl.multiple_of(device * rows, rows), rows)

    arrays = ((k_ref, k_all), (v_ref, v_all), (q_ref, q_all))

    @pl.when(low)
    def _():
        pltpu.make_async_copy(first_keys, first_keys, first_done).wait()

    def send_input(device, slot, which):
        source, target = arrays[which]

        def send(piece):
            pltpu.make_async_remote_copy(
                src_ref=piece,
                dst_ref=target.at[slot, part(me)],
                send_sem=in_send.at[slot, which],
                recv_sem=in_recv.at[slot, which],
                **at_space(device),
            ).start()

        piece = source.at[:, lanes(device * grouped + slot)]
        if slot == 0 and which == 0:

            @pl.when(low)
            def _():
                send(first_keys.at[device])

            @pl.when(jnp.logical_not(low))
            def _():
                send(piece)
        else:
            send(piece)

    def send_chip(position, slot, which):
        there, same, opposite = targets[position]

        @pl.when(there != chip)
        def _():
            send_input(same, slot, which)

        send_input(opposite, slot, which)

    for slot in range(grouped):
        known = chips - 1 if slot == 0 else chips
        for which in range(len(arrays)):
            for position in range(known):
                send_chip(position, slot, which)
        if slot == 0:
            for device in (count - 2, count - 1):

                @pl.when(place(device) > rank)
                def _():
                    pl.semaphore_wait(ready.at[device], 1)

            for which in range(len(arrays)):
                send_chip(chips - 1, slot, which)

    for slot in range(grouped):
        for which, (source, target) in enumerate(arrays):
            pltpu.make_async_copy(
                source.at[:, lanes(me * grouped + slot)],
                target.at[slot, part(me)],
                in_recv.at[slot, which],
            ).start()

    for copy in small:
        copy.start()

    @pl.when(is_hub)
    def _():
        for step in range(1, blocks):
            pl.semaphore_signal(column_ready, inc=1, **at_tm(step))
        pl.semaphore_wait(column_ready, blocks - 1)
        for other in range(count):
            if place(other) > 0:
                pl.semaphore_signal(all_ready, inc=1, **at_space(other))

    @pl.when(rank > 0)
    def _():
        pl.semaphore_wait(all_ready, 1)

    def arrived(slot, which):
        whole = arrays[which][1].at[slot]
        pltpu.make_async_copy(whole, whole, in_recv.at[slot, which]).wait()

    def give_back(slot, device, done=None):
        pltpu.make_async_remote_copy(
            src_ref=outcome.at[slot, part(device)],
            dst_ref=out_ref.at[:, lanes(me * grouped + slot)],
            send_sem=out_send.at[slot] if done is None else done,
            recv_sem=out_recv.at[0],
            **at_space(device),
        ).start()

    far_chips = [jnp.where(low, half + k, k) for k in range(half)]
    near_chips = [half * jnp.where(low, 0, 1) + k for k in range(half)]

    def give_far(slot, which):
        for digit in range(2):
            give_back(
                slot, 2 * far_chips[which] + digit,
                first_send.at[slot // (grouped - 1)] if which == 0 else None,
            )

    at_end = jnp.logical_or(chip == 0, chip == chips - 1)

    def give_first():
        for earlier in range(grouped - 2):
            give_far(earlier, 0)
            give_far(earlier, 1)

    def give_earlier():
        give_far(grouped - 2, 0)
        give_back(grouped - 2, 2 * far_chips[1])

        @pl.when(core == 0)
        def _():
            give_back(grouped - 2, 2 * far_chips[1] + 1)

    def give_near(slot):
        for there in near_chips:

            @pl.when(there != chip)
            def _():
                give_back(slot, 2 * there)
                give_back(slot, 2 * there + 1)

        give_back(slot, 2 * chip + 1 - core)

    for copy in small:
        copy.wait()
    level = jnp.full((8, depth), noise_ref[0], jnp.int32).astype(jnp.float32)
    for slot in range(grouped):
        head = me * grouped + slot
        power = jnp.full((8, depth), power_ref[head], jnp.int32).astype(jnp.float32)
        rate = jnp.exp2(-(power * (0.25 + 1.75 * level / LEVELS)) / blocks)
        arrived(slot, 0)
        arrived(slot, 1)
        fresh = lax.dot_general(
            k_all[slot], v_all[slot], (((0,), (0,)), ((), ())), preferred_element_type=jnp.float32
        )
        fresh_mine[slot, 0:depth, :] = fresh / total_rows
        fresh_mine[slot, depth : depth + 8, :] = rate
        for step in range(1, blocks):
            pltpu.make_async_remote_copy(
                src_ref=fresh_mine.at[slot],
                dst_ref=fresh_got.at[slot, step - 1],
                send_sem=fresh_send.at[slot],
                recv_sem=fresh_recv.at[slot],
                **at_tm(step),
            ).start()
        arrived(slot, 2)
        if slot == grouped - 1:
            @pl.when(at_end)
            def _():
                give_first()
                give_earlier()

        landed = fresh_got.at[slot]
        pltpu.make_async_copy(landed, landed, fresh_recv.at[slot]).wait()
        carried = jnp.zeros((depth, depth), jnp.float32)
        for step in range(blocks - 1, 0, -1):
            longer = (
                fresh_got[slot, step - 1, depth : depth + 1, :] * carried
                + fresh_got[slot, step - 1, 0:depth, :]
            )
            carried = jnp.where(now - step >= 0, longer, carried)
        state = (rate[0:1, :] * carried).astype(jnp.bfloat16)
        gain_row = gain_ref[pl.ds(head, 1), :]

        def attend(first_chip):
            span = pl.ds(pl.multiple_of(first_chip * 2 * rows, 2 * half * rows), 2 * half * rows)
            query = q_all[slot, span, :]
            scores = lax.dot_general(
                query, k_all[slot], (((1,), (1,)), ((), ())), preferred_element_type=jnp.float32
            ) * factor
            weights = jnp.exp(scores - jnp.max(scores, axis=1, keepdims=True))
            row_total = jnp.sum(weights, axis=1, keepdims=True)
            numerator = jnp.dot(
                weights.astype(jnp.bfloat16), v_all[slot], preferred_element_type=jnp.float32
            )
            before = jnp.dot(query, state, preferred_element_type=jnp.float32) * factor
            mixed = numerator / row_total + before
            scale = lax.rsqrt(jnp.mean(mixed * mixed, axis=1, keepdims=True) + epsilon)
            outcome[slot, span, :] = (mixed * scale * gain_row).astype(jnp.bfloat16)

        attend(half * jnp.where(low, 1, 0))
        if slot == grouped - 1:
            give_far(slot, 0)
        attend(near_chips[0])
        give_near(slot)
        if slot == grouped - 3:
            @pl.when(jnp.logical_not(at_end))
            def _():
                give_first()

        if slot == grouped - 2:
            @pl.when(jnp.logical_not(at_end))
            def _():
                give_earlier()

        if slot == grouped - 1:
            @pl.when(jnp.logical_and(chip == half, core == 1))
            def _():
                first = outcome.at[0, pl.ds(0, 2 * rows * (grouped - 1))]
                pltpu.make_async_copy(first, first, first_send.at[0]).wait()

            @pl.when(jnp.logical_not(core == 0))
            def _():
                give_back(grouped - 2, 2 * far_chips[1] + 1)

            give_far(slot, 1)
        pltpu.make_async_copy(
            outcome.at[slot, part(me)], out_ref.at[:, lanes(head)], out_recv.at[0]
        ).start()

    @pl.when(jnp.logical_not(jnp.logical_and(chip == half, core == 1)))
    def _():
        first = outcome.at[0, pl.ds(0, 2 * rows * (grouped - 1))]
        pltpu.make_async_copy(first, first, first_send.at[0]).wait()

    last = outcome.at[0, pl.ds(0, 2 * rows)]
    pltpu.make_async_copy(last, last, first_send.at[1]).wait()
    for slot in range(grouped):
        for which in range(len(arrays)):
            sent = arrays[which][1].at[slot, pl.ds(0, total_rows - rows)]
            pltpu.make_async_copy(sent, sent, in_send.at[slot, which]).wait()
        landed = fresh_got.at[slot]
        pltpu.make_async_copy(landed, landed, fresh_send.at[slot]).wait()
        returned = outcome.at[slot, pl.ds(0, total_rows - 3 * rows)]
        pltpu.make_async_copy(returned, returned, out_send.at[slot]).wait()
    pltpu.make_async_copy(out_ref, out_ref, out_recv.at[0]).wait()


def fused(queries, key_rows, value_rows, noise_level, decay_power, head_gain):
    count, blocks = lax.axis_size("space"), lax.axis_size("tm")
    rows, width = queries.shape[1:]
    heads_total, depth = head_gain.shape
    grouped = heads_total // count
    held = [
        pltpu.with_memory_space_constraint(operand, pltpu.HBM)
        for operand in (queries[0], key_rows[0], value_rows[0], decay_power, head_gain)
    ]
    held.insert(3, noise_level)
    gathered = pltpu.VMEM((grouped, count * rows, depth), jnp.bfloat16)
    dma = pltpu.SemaphoreType.DMA
    out = pl.pallas_call(
        functools.partial(fused_kernel, count, blocks),
        out_shape=jax.ShapeDtypeStruct((rows, width), jnp.bfloat16),
        in_specs=[pl.BlockSpec(memory_space=pl.ANY)] * len(held),
        out_specs=pl.BlockSpec(memory_space=pl.ANY),
        scratch_shapes=[
            pltpu.SMEM(noise_level.shape, jnp.int32),
            pltpu.SMEM(decay_power.shape, jnp.int32),
            pltpu.VMEM(head_gain.shape, jnp.float32),
            dma((3,)),
            gathered,
            gathered,
            gathered,
            gathered,
            pltpu.VMEM((grouped, depth + 8, depth), jnp.float32),
            pltpu.VMEM((grouped, blocks - 1, depth + 8, depth), jnp.float32),
            dma((grouped, 3)),
            dma((grouped, 3)),
            dma((grouped,)),
            dma((1,)),
            dma((grouped,)),
            dma((grouped,)),
            pltpu.VMEM((count, rows, depth), jnp.bfloat16),
            pltpu.SemaphoreType.DMA,
            dma((2,)),
            pltpu.SemaphoreType.REGULAR((count,)),
            pltpu.SemaphoreType.REGULAR,
            pltpu.SemaphoreType.REGULAR,
        ],
        compiler_params=pltpu.CompilerParams(collective_id=0, has_side_effects=True, vmem_limit_bytes=VMEM_GRANT),
        name="heads_exchange",
    )(*held)
    return out[None]


def body(queries, key_rows, value_rows, noise_level, decay_power, head_gain):
    heads_total = decay_power.shape[0]
    depth = head_gain.shape[1]
    local_rows = queries.shape[1]
    quarters = lax.axis_size("space") // HGROUPS
    grouped = heads_total // HGROUPS
    query_items = spread_items(queries[0], quarters, heads_total, depth)
    keys_sent = copied_items(key_rows[0], quarters, heads_total, depth)
    values_sent = copied_items(value_rows[0], quarters, heads_total, depth)
    query_got, keys_got, values_got = (
        lax.all_to_all(query_items, "space", split_axis=0, concat_axis=1, tiled=True),
        lax.all_to_all(keys_sent, "space", split_axis=0, concat_axis=1, tiled=True),
        lax.all_to_all(values_sent, "space", split_axis=0, concat_axis=1, tiled=True),
    )
    key_count = keys_got.shape[1]
    fresh = (
        jnp.einsum("inh,ine->ihe", keys_got, values_got, preferred_element_type=jnp.float32)
        / key_count
    )
    group_index = lax.axis_index("space") % HGROUPS
    powers = lax.dynamic_slice_in_dim(decay_power, group_index * grouped, grouped).astype(
        jnp.float32
    )
    level_now = noise_level[0].astype(jnp.float32)
    block_count = lax.axis_size("tm")
    rate = jnp.exp2(-(powers * (0.25 + 1.75 * level_now / LEVELS)) / block_count)
    zeros_state = jnp.zeros_like(fresh)
    unused_rate, before = carried_in(
        (rate, fresh), "tm", compose, (jnp.ones_like(rate), zeros_state)
    )
    state = (rate[:, None, None] * before).astype(jnp.bfloat16)
    gain_rows = lax.dynamic_slice_in_dim(head_gain, group_index * grouped, grouped)
    outcome = lax.map(attend_head, (query_got, keys_got, values_got, state, gain_rows))
    returned = lax.all_to_all(outcome, "space", split_axis=1, concat_axis=0, tiled=True)
    part_rows = local_rows // quarters
    restored = returned.reshape(quarters, heads_total, part_rows, depth).transpose(0, 2, 1, 3)
    return restored.reshape(1, local_rows, heads_total * depth)


def solution(mesh):
    in_specs = (
        P("tm", "space", None),
        P("tm", "space", None),
        P("tm", "space", None),
        P("tm"),
        P(),
        P(),
    )
    out_specs = P("tm", "space", None)
    step = fused if mesh.shape["space"] == HGROUPS else body
    return jax.shard_map(step, mesh=mesh, in_specs=in_specs, out_specs=out_specs, check_vma=False)
```

```python
import functools

import jax
import jax.numpy as jnp
from jax import lax
from jax.experimental import pallas as pl
from jax.experimental.pallas import tpu as pltpu
from jax.sharding import PartitionSpec as P

LEVELS = 1000
HGROUPS = 8
VMEM_GRANT = 32 * 2**20


epsilon = 1e-06


def carried_in(value, axis, join, neutral):
    count, mine = (lax.axis_size(axis), lax.axis_index(axis))
    pieces = jax.tree.map(lambda part: lax.all_gather(part, axis), value)
    so_far = jax.tree.map(
        lambda part, zero: jnp.full_like(part, 0) + jnp.asarray(zero, part.dtype), value, neutral
    )

    def lap(position, so_far):
        longer = join(so_far, jax.tree.map(lambda part: part[position], pieces))
        return jax.tree.map(lambda new, old: jnp.where(position < mine, new, old), longer, so_far)

    return lax.fori_loop(0, count - 1, lap, so_far)


def spread_items(block, quarters, heads_total, depth):
    part_rows = block.shape[0] // quarters
    shaped = block.reshape(quarters, part_rows, heads_total, depth).transpose(0, 2, 1, 3)
    return shaped.reshape(quarters * heads_total, part_rows, depth)


def copied_items(block, quarters, heads_total, depth):
    every = block.reshape(block.shape[0], heads_total, depth).transpose(1, 0, 2)
    copied = jnp.broadcast_to(every[None], (quarters,) + every.shape)
    return copied.reshape(quarters * heads_total, block.shape[0], depth)


def attend_head(bundle):
    query, key_item, value_item, state, gain_row = bundle
    factor = query.shape[1] ** (-0.5)
    scores = jnp.dot(query, key_item.T, preferred_element_type=jnp.float32) * factor
    row_top = jnp.max(scores, axis=1, keepdims=True)
    weights = jnp.exp(scores - row_top)
    row_total = jnp.sum(weights, axis=1, keepdims=True)
    numerator = jnp.dot(
        weights.astype(jnp.bfloat16), value_item, preferred_element_type=jnp.float32
    )
    carried = jnp.dot(query, state, preferred_element_type=jnp.float32) * factor
    mixed = numerator / row_total + carried
    normed = mixed * lax.rsqrt(jnp.mean(mixed * mixed, axis=1, keepdims=True) + epsilon) * gain_row
    return normed.astype(jnp.bfloat16)


def compose(earlier, later):
    return (earlier[0] * later[0], later[0][:, None, None] * earlier[1] + later[1])


MESH = pl.DeviceIdType.MESH


def fused_kernel(
    count, blocks, q_ref, k_ref, v_ref, noise_hbm, power_hbm, gain_hbm, out_ref,
    noise_ref, power_ref, gain_ref, small_done,
    q_all, k_all, v_all, outcome, fresh_mine, fresh_got,
    in_send, in_recv, out_send, out_recv, fresh_send, fresh_recv,
    first_keys, first_done, first_send, ready, column_ready, all_ready,
):
    rows = q_ref.shape[0]
    depth = gain_ref.shape[1]
    grouped = q_all.shape[0]
    total_rows = count * rows
    factor = depth ** (-0.5)
    me, now = lax.axis_index("space"), lax.axis_index("tm")
    chips, half = count // 2, count // 4
    chip, core = me // 2, me % 2

    def place(device):
        return device + 1 - 2 * (device % 2)

    rank = place(me)

    def at_space(device):
        return {"device_id": {"space": device}, "device_id_type": MESH}

    def at_tm(step):
        return {"device_id": {"tm": lax.rem(now + step, blocks)}, "device_id_type": MESH}

    low = chip < half
    targets = []
    for k in range(chips):
        if k == 0:
            below = chip
        elif k < half:
            below = k - 1 + jnp.where(k - 1 >= chip, 1, 0)
        else:
            below = k
        above = half - 1 - k if k < half else k
        there = jnp.where(low, below, above)
        targets.append((there, 2 * there + core, 2 * there + 1 - core))

    small = [
        pltpu.make_async_copy(held, here, small_done.at[index])
        for index, (held, here) in enumerate(
            ((noise_hbm, noise_ref), (power_hbm, power_ref), (gain_hbm, gain_ref))
        )
    ]

    barrier = pltpu.get_barrier_semaphore()
    is_hub = rank == 0
    is_last = chip == chips - 1
    for other in range(count - 1, -1, -1):

        @pl.when(jnp.logical_and(me != other, jnp.logical_or(jnp.logical_not(is_last), place(other) > rank)))
        def _():
            pl.semaphore_signal(barrier, inc=1, **at_space(other))

    @pl.when(is_hub)
    def _():
        for step in range(1, blocks):
            pl.semaphore_signal(barrier, inc=1, **at_tm(step))

    @pl.when(low)
    def _():
        for device in range(count):
            pltpu.make_async_copy(
                k_ref.at[:, pl.ds(device * grouped * depth, depth)], first_keys.at[device], first_done
            ).start()

    pl.semaphore_wait(
        barrier, jnp.where(is_last, rank, count - 3 + jnp.where(is_hub, blocks - 1, 0))
    )

    @pl.when(is_last)
    def _():
        for other in range(count):

            @pl.when(place(other) < rank)
            def _():
                pl.semaphore_signal(ready.at[me], inc=1, **at_space(other))

    def lanes(head):
        return pl.ds(pl.multiple_of(head * depth, depth), depth)

    def part(device):
        return pl.ds(pl.multiple_of(device * rows, rows), rows)

    arrays = ((k_ref, k_all), (v_ref, v_all), (q_ref, q_all))

    @pl.when(low)
    def _():
        pltpu.make_async_copy(first_keys, first_keys, first_done).wait()

    def send_input(device, slot, which):
        source, target = arrays[which]

        def send(piece):
            pltpu.make_async_remote_copy(
                src_ref=piece,
                dst_ref=target.at[slot, part(me)],
                send_sem=in_send.at[slot, which],
                recv_sem=in_recv.at[slot, which],
                **at_space(device),
            ).start()

        piece = source.at[:, lanes(device * grouped + slot)]
        if slot == 0 and which == 0:

            @pl.when(low)
            def _():
                send(first_keys.at[device])

            @pl.when(jnp.logical_not(low))
            def _():
                send(piece)
        else:
            send(piece)

    def send_chip(position, slot, which):
        there, same, opposite = targets[position]

        @pl.when(there != chip)
        def _():
            send_input(same, slot, which)

        send_input(opposite, slot, which)

    for slot in range(grouped):
        known = chips - 1 if slot == 0 else chips
        if slot == 0:

            @pl.when(jnp.logical_not(low))
            def _():
                for which in range(len(arrays)):
                    for position in range(half):
                        send_chip(position, slot, which)
                for which in range(len(arrays)):
                    for position in range(half, known):
                        send_chip(position, slot, which)

            @pl.when(low)
            def _():
                for which in range(len(arrays)):
                    for position in range(known):
                        send_chip(position, slot, which)
        else:
            for which in range(len(arrays)):
                for position in range(known):
                    send_chip(position, slot, which)
        if slot == 0:
            for device in (count - 2, count - 1):

                @pl.when(place(device) > rank)
                def _():
                    pl.semaphore_wait(ready.at[device], 1)

            for which in range(len(arrays)):
                send_chip(chips - 1, slot, which)

    for slot in range(grouped):
        for which, (source, target) in enumerate(arrays):
            pltpu.make_async_copy(
                source.at[:, lanes(me * grouped + slot)],
                target.at[slot, part(me)],
                in_recv.at[slot, which],
            ).start()

    for copy in small:
        copy.start()

    @pl.when(is_hub)
    def _():
        for step in range(1, blocks):
            pl.semaphore_signal(column_ready, inc=1, **at_tm(step))
        pl.semaphore_wait(column_ready, blocks - 1)
        for other in range(count):
            if place(other) > 0:
                pl.semaphore_signal(all_ready, inc=1, **at_space(other))

    @pl.when(rank > 0)
    def _():
        pl.semaphore_wait(all_ready, 1)

    def arrived(slot, which):
        whole = arrays[which][1].at[slot]
        pltpu.make_async_copy(whole, whole, in_recv.at[slot, which]).wait()

    def give_back(slot, device, done=None):
        pltpu.make_async_remote_copy(
            src_ref=outcome.at[slot, part(device)],
            dst_ref=out_ref.at[:, lanes(me * grouped + slot)],
            send_sem=out_send.at[slot] if done is None else done,
            recv_sem=out_recv.at[0],
            **at_space(device),
        ).start()

    far_chips = [jnp.where(low, half + k, k) for k in range(half)]
    near_chips = [half * jnp.where(low, 0, 1) + k for k in range(half)]

    def give_far(slot, which):
        for digit in range(2):
            give_back(
                slot, 2 * far_chips[which] + digit,
                first_send.at[slot // (grouped - 1)] if which == 0 else None,
            )

    at_end = jnp.logical_or(chip == 0, chip == chips - 1)

    def give_earlier():
        for earlier in range(grouped - 1):
            give_far(earlier, 0)
        for earlier in range(grouped - 2):
            give_far(earlier, 1)
        give_back(grouped - 2, 2 * far_chips[1])

        @pl.when(core == 0)
        def _():
            give_back(grouped - 2, 2 * far_chips[1] + 1)

    def give_near(slot):
        for there in near_chips:

            @pl.when(there != chip)
            def _():
                give_back(slot, 2 * there)
                give_back(slot, 2 * there + 1)

        give_back(slot, 2 * chip + 1 - core)

    for copy in small:
        copy.wait()
    level = jnp.full((8, depth), noise_ref[0], jnp.int32).astype(jnp.float32)
    for slot in range(grouped):
        head = me * grouped + slot
        power = jnp.full((8, depth), power_ref[head], jnp.int32).astype(jnp.float32)
        rate = jnp.exp2(-(power * (0.25 + 1.75 * level / LEVELS)) / blocks)
        arrived(slot, 0)
        arrived(slot, 1)
        fresh = lax.dot_general(
            k_all[slot], v_all[slot], (((0,), (0,)), ((), ())), preferred_element_type=jnp.float32
        )
        fresh_mine[slot, 0:depth, :] = fresh / total_rows
        fresh_mine[slot, depth : depth + 8, :] = rate
        for step in range(1, blocks):
            pltpu.make_async_remote_copy(
                src_ref=fresh_mine.at[slot],
                dst_ref=fresh_got.at[slot, step - 1],
                send_sem=fresh_send.at[slot],
                recv_sem=fresh_recv.at[slot],
                **at_tm(step),
            ).start()
        arrived(slot, 2)
        if slot == grouped - 1:
            @pl.when(at_end)
            def _():
                give_earlier()

        landed = fresh_got.at[slot]
        pltpu.make_async_copy(landed, landed, fresh_recv.at[slot]).wait()
        carried = jnp.zeros((depth, depth), jnp.float32)
        for step in range(blocks - 1, 0, -1):
            longer = (
                fresh_got[slot, step - 1, depth : depth + 1, :] * carried
                + fresh_got[slot, step - 1, 0:depth, :]
            )
            carried = jnp.where(now - step >= 0, longer, carried)
        state = (rate[0:1, :] * carried).astype(jnp.bfloat16)
        gain_row = gain_ref[pl.ds(head, 1), :]

        def attend(first_chip):
            span = pl.ds(pl.multiple_of(first_chip * 2 * rows, 2 * half * rows), 2 * half * rows)
            query = q_all[slot, span, :]
            scores = lax.dot_general(
                query, k_all[slot], (((1,), (1,)), ((), ())), preferred_element_type=jnp.float32
            ) * factor
            weights = jnp.exp(scores - jnp.max(scores, axis=1, keepdims=True))
            row_total = jnp.sum(weights, axis=1, keepdims=True)
            numerator = jnp.dot(
                weights.astype(jnp.bfloat16), v_all[slot], preferred_element_type=jnp.float32
            )
            before = jnp.dot(query, state, preferred_element_type=jnp.float32) * factor
            mixed = numerator / row_total + before
            scale = lax.rsqrt(jnp.mean(mixed * mixed, axis=1, keepdims=True) + epsilon)
            outcome[slot, span, :] = (mixed * scale * gain_row).astype(jnp.bfloat16)

        attend(half * jnp.where(low, 1, 0))
        if slot == grouped - 1:
            give_far(slot, 0)
        attend(near_chips[0])
        give_near(slot)
        if slot == grouped - 2:
            @pl.when(jnp.logical_not(at_end))
            def _():
                give_earlier()

        if slot == grouped - 1:
            @pl.when(jnp.logical_not(low))
            def _():
                first = outcome.at[0, pl.ds(0, 2 * rows * (grouped - 1))]
                pltpu.make_async_copy(first, first, first_send.at[0]).wait()

            @pl.when(jnp.logical_not(core == 0))
            def _():
                give_back(grouped - 2, 2 * far_chips[1] + 1)

            give_far(slot, 1)
        pltpu.make_async_copy(
            outcome.at[slot, part(me)], out_ref.at[:, lanes(head)], out_recv.at[0]
        ).start()

    @pl.when(low)
    def _():
        first = outcome.at[0, pl.ds(0, 2 * rows * (grouped - 1))]
        pltpu.make_async_copy(first, first, first_send.at[0]).wait()

    last = outcome.at[0, pl.ds(0, 2 * rows)]
    pltpu.make_async_copy(last, last, first_send.at[1]).wait()
    for slot in range(grouped):
        for which in range(len(arrays)):
            sent = arrays[which][1].at[slot, pl.ds(0, total_rows - rows)]
            pltpu.make_async_copy(sent, sent, in_send.at[slot, which]).wait()
        landed = fresh_got.at[slot]
        pltpu.make_async_copy(landed, landed, fresh_send.at[slot]).wait()
        returned = outcome.at[slot, pl.ds(0, total_rows - 3 * rows)]
        pltpu.make_async_copy(returned, returned, out_send.at[slot]).wait()
    pltpu.make_async_copy(out_ref, out_ref, out_recv.at[0]).wait()


def fused(queries, key_rows, value_rows, noise_level, decay_power, head_gain):
    count, blocks = lax.axis_size("space"), lax.axis_size("tm")
    rows, width = queries.shape[1:]
    heads_total, depth = head_gain.shape
    grouped = heads_total // count
    held = [
        pltpu.with_memory_space_constraint(operand, pltpu.HBM)
        for operand in (queries[0], key_rows[0], value_rows[0], decay_power, head_gain)
    ]
    held.insert(3, noise_level)
    gathered = pltpu.VMEM((grouped, count * rows, depth), jnp.bfloat16)
    dma = pltpu.SemaphoreType.DMA
    out = pl.pallas_call(
        functools.partial(fused_kernel, count, blocks),
        out_shape=jax.ShapeDtypeStruct((rows, width), jnp.bfloat16),
        in_specs=[pl.BlockSpec(memory_space=pl.ANY)] * len(held),
        out_specs=pl.BlockSpec(memory_space=pl.ANY),
        scratch_shapes=[
            pltpu.SMEM(noise_level.shape, jnp.int32),
            pltpu.SMEM(decay_power.shape, jnp.int32),
            pltpu.VMEM(head_gain.shape, jnp.float32),
            dma((3,)),
            gathered,
            gathered,
            gathered,
            gathered,
            pltpu.VMEM((grouped, depth + 8, depth), jnp.float32),
            pltpu.VMEM((grouped, blocks - 1, depth + 8, depth), jnp.float32),
            dma((grouped, 3)),
            dma((grouped, 3)),
            dma((grouped,)),
            dma((1,)),
            dma((grouped,)),
            dma((grouped,)),
            pltpu.VMEM((count, rows, depth), jnp.bfloat16),
            pltpu.SemaphoreType.DMA,
            dma((2,)),
            pltpu.SemaphoreType.REGULAR((count,)),
            pltpu.SemaphoreType.REGULAR,
            pltpu.SemaphoreType.REGULAR,
        ],
        compiler_params=pltpu.CompilerParams(collective_id=0, has_side_effects=True, vmem_limit_bytes=VMEM_GRANT),
        name="heads_exchange",
    )(*held)
    return out[None]


def body(queries, key_rows, value_rows, noise_level, decay_power, head_gain):
    heads_total = decay_power.shape[0]
    depth = head_gain.shape[1]
    local_rows = queries.shape[1]
    quarters = lax.axis_size("space") // HGROUPS
    grouped = heads_total // HGROUPS
    query_items = spread_items(queries[0], quarters, heads_total, depth)
    keys_sent = copied_items(key_rows[0], quarters, heads_total, depth)
    values_sent = copied_items(value_rows[0], quarters, heads_total, depth)
    query_got, keys_got, values_got = (
        lax.all_to_all(query_items, "space", split_axis=0, concat_axis=1, tiled=True),
        lax.all_to_all(keys_sent, "space", split_axis=0, concat_axis=1, tiled=True),
        lax.all_to_all(values_sent, "space", split_axis=0, concat_axis=1, tiled=True),
    )
    key_count = keys_got.shape[1]
    fresh = (
        jnp.einsum("inh,ine->ihe", keys_got, values_got, preferred_element_type=jnp.float32)
        / key_count
    )
    group_index = lax.axis_index("space") % HGROUPS
    powers = lax.dynamic_slice_in_dim(decay_power, group_index * grouped, grouped).astype(
        jnp.float32
    )
    level_now = noise_level[0].astype(jnp.float32)
    block_count = lax.axis_size("tm")
    rate = jnp.exp2(-(powers * (0.25 + 1.75 * level_now / LEVELS)) / block_count)
    zeros_state = jnp.zeros_like(fresh)
    unused_rate, before = carried_in(
        (rate, fresh), "tm", compose, (jnp.ones_like(rate), zeros_state)
    )
    state = (rate[:, None, None] * before).astype(jnp.bfloat16)
    gain_rows = lax.dynamic_slice_in_dim(head_gain, group_index * grouped, grouped)
    outcome = lax.map(attend_head, (query_got, keys_got, values_got, state, gain_rows))
    returned = lax.all_to_all(outcome, "space", split_axis=1, concat_axis=0, tiled=True)
    part_rows = local_rows // quarters
    restored = returned.reshape(quarters, heads_total, part_rows, depth).transpose(0, 2, 1, 3)
    return restored.reshape(1, local_rows, heads_total * depth)


def solution(mesh):
    in_specs = (
        P("tm", "space", None),
        P("tm", "space", None),
        P("tm", "space", None),
        P("tm"),
        P(),
        P(),
    )
    out_specs = P("tm", "space", None)
    step = fused if mesh.shape["space"] == HGROUPS else body
    return jax.shard_map(step, mesh=mesh, in_specs=in_specs, out_specs=out_specs, check_vma=False)
```
